512 devices in a mesh: ctx: 32 (over z, core), tp: 16 (over x, y).
Axes of the slice: x: 4, y: 4, z: 16, core: 2. Of those that a mesh axis runs over, the one named last changes fastest.
Arguments:
- queries: bfloat16 [8192, 8192], P('ctx', 'tp'), may hold values from -6 to 6
- keys: bfloat16 [8192, 8192], P('ctx', 'tp'), may hold values from -0.0625 to 0.0625
- values: bfloat16 [8192, 8192], P('ctx', 'tp'), may hold values from -6 to 6
- log_keep: float32 [64, 8192], P('tp', 'ctx'), may hold values from -1 to 0, as said below
- state_in: float32 [64, 128, 128], P('tp'), may hold values from -6 to 6
- norm_gain: float32 [8192], P('tp'), may hold values from 0.1 to 1.9
- out_weight: bfloat16 [8192, 6144], P('tp', 'ctx'), may hold values from -0.125 to 0.125
Outputs:
- normed: bfloat16 [8192, 8192], P('ctx', 'tp')
- state_out: float32 [64, 128, 128], P('tp', 'ctx')
- layer_out: bfloat16 [8192, 6144], P('ctx', 'tp')
The draws below stay inside these ranges and needn't reach their ends.
Inputs may be any that keep to these rules, and one draw needn't show every extreme that they name: `log_keep`: every entry is a logarithm of a keep factor, so at most 0.
All inputs are finite; a program needn't handle non-finite values.
Results may differ from the reference program's by a relative error of at most 0.014.
Values may be sent and summed in bfloat16 or wider, within the bound.
No kernel may reach another device: no remote copies, remote signals or barrier semaphores. Data moves between devices by JAX's collectives and lax.ppermute only.
A program may use at most 64 MiB of HBM per device.

```python
import jax
import jax.numpy as jnp
from jax import lax

H = 64
DH = 128
D = 6144
SPAN = 256
TOKENS = 8192
N_TP = 16


def draw_log_keep(key, part):
    k_fast, k_quick, k_slow, k_spots, k_depth = jax.random.split(key, 5)
    share = 0.5
    fast = jax.random.bernoulli(k_fast, share, (H,))
    quick_rate = jnp.exp(jax.random.uniform(k_quick, (H,), jnp.float32, jnp.log(1.0 / 50.0), jnp.log(1.0 / 30.0)))
    slow_rate = jnp.exp(jax.random.uniform(k_slow, (H,), jnp.float32, jnp.log(0.05), jnp.log(0.5))) / TOKENS
    decay_rate = jnp.where(fast, quick_rate, slow_rate)
    token_positions = jax.random.randint(k_spots, (2, H), 0, TOKENS)
    layer_depth = jax.random.uniform(k_depth, (2, H), jnp.float32, jnp.log(0.5), jnp.log(0.8))
    part_positions = jnp.arange(TOKENS)
    block_length = jnp.where(part_positions[None, :] == token_positions[0][:, None], layer_depth[0][:, None], 0.0)
    block_length = block_length + jnp.where(part_positions[None, :] == token_positions[1][:, None], layer_depth[1][:, None], 0.0)
    return jnp.maximum(block_length - decay_rate[:, None], -1.0).astype(jnp.float32)


def spiked(array, rng, source, target, parts, factor):
    def block_of(position):
        return (jnp.arange(array.shape[position]) // (array.shape[position] // parts)).reshape((-1,) + (1,) * (array.ndim - 1 - position))

    near = jax.random.permutation(rng, parts)[block_of(target)]
    far = (block_of(target) + parts // 2) % parts
    return jnp.where((block_of(source) == near) | (block_of(source) == far), factor * array, array)


def block_scale(rng, dims, cuts, least, largest):
    factor_of = 1.0
    for position, parts in cuts:
        draws = jax.random.uniform(jax.random.fold_in(jax.random.fold_in(rng, 6), position), (parts,), jnp.float32, least / len(cuts), largest / len(cuts))
        factor_of = factor_of * jnp.repeat(jnp.exp(draws), dims[position] // parts).reshape((-1,) + (1,) * (len(dims) - 1 - position))
    return factor_of


def gaussian(own_key, dims, scale, limit, cuts=(), kind=jnp.bfloat16):
    array = scale * jax.random.normal(own_key, dims, jnp.float32)
    if cuts:
        array = array * block_scale(own_key, dims, cuts, -0.22, 0.18)
    return jnp.clip(array, -limit, limit).astype(kind)


def noise_with(own_key, dims, scale, reach, pieces, heavy, kind=jnp.bfloat16):
    result = scale * jax.random.normal(own_key, dims, jnp.float32)
    if pieces:
        result = result * block_scale(own_key, dims, pieces, -0.22, 0.18)
    return jnp.clip(spiked(result, jax.random.fold_in(own_key, 3), *heavy), -reach, reach).astype(kind)


def setup_inputs(seed: int = 0) -> dict:
    key_of = jax.random.split(jax.random.key(seed), 8)
    return {
        "queries": gaussian(key_of[0], (TOKENS, H * DH), 1.0, 6.0, ((0, 32), (1, 16))),
        "keys": gaussian(key_of[1], (TOKENS, H * DH), TOKENS ** -0.5, 0.0625, ((0, 32), (1, 16))),
        "values": gaussian(key_of[2], (TOKENS, H * DH), 1.0, 6.0, ((0, 32), (1, 16))),
        "log_keep": draw_log_keep(jax.random.fold_in(key_of[7], 71), 0),
        "state_in": gaussian(key_of[4], (H, DH, DH), 1.0, 6.0, ((0, 16),), jnp.float32),
        "norm_gain": jnp.clip(1.0 + 0.18 * jax.random.normal(key_of[5], (H * DH,), jnp.float32), 0.1, 1.9),
        "out_weight": noise_with(key_of[6], (H * DH, D), (H * DH) ** -0.5, 0.125, ((0, 16), (1, 32)), (0, 1, 32, 2.75)),
    }


def reference(queries, keys, values, log_keep, state_in, norm_gain, out_weight):
    blocks = TOKENS // SPAN
    q_all = queries.reshape(blocks, SPAN, H, DH)
    k_all = keys.reshape(blocks, SPAN, H, DH)
    v_all = values.reshape(blocks, SPAN, H, DH)
    logs = log_keep.reshape(H, blocks, SPAN).transpose(1, 0, 2)
    causal = jnp.tril(jnp.ones((SPAN, SPAN), dtype=bool))

    def advance(state, item):
        q_blk, k_blk, v_blk, log_blk = item
        q_f = q_blk.astype(jnp.float32)
        k_f = k_blk.astype(jnp.float32)
        v_f = v_blk.astype(jnp.float32)
        within = jnp.cumsum(log_blk, axis=1)
        spread = within[:, :, None] - within[:, None, :]
        decay = jnp.where(causal[None], jnp.exp(jnp.minimum(spread, 0.0)), 0.0)
        scores = jnp.einsum('shd,thd->hst', q_f, k_f)
        weights = lax.optimization_barrier((scores * decay).astype(jnp.bfloat16))
        intra = jnp.einsum('hst,thd->shd', weights.astype(jnp.float32), v_f)
        start = lax.optimization_barrier(state.astype(jnp.bfloat16))
        inter = jnp.einsum('shd,hde->she', q_f, start.astype(jnp.float32)) * jnp.exp(within).T[:, :, None]
        total = within[:, -1]
        keys_decayed = lax.optimization_barrier((k_f * jnp.exp(total[:, None] - within).T[:, :, None]).astype(jnp.bfloat16))
        increment = jnp.einsum('shd,she->hde', keys_decayed.astype(jnp.float32), v_f)
        state = jnp.exp(total)[:, None, None] * state + increment
        return (state, intra + inter)
    state_out, outs = lax.scan(advance, state_in, (q_all, k_all, v_all, logs))
    attended = outs.reshape(TOKENS, H * DH)
    mean_square = lax.optimization_barrier(jnp.mean(attended * attended, axis=1))
    normed = (attended * lax.rsqrt(mean_square + 1e-06)[:, None] * norm_gain).astype(jnp.bfloat16)
    group = H * DH // N_TP
    normed_parts = normed.reshape(TOKENS, N_TP, group).transpose(1, 0, 2)
    weight_parts = out_weight.reshape(N_TP, group, D)

    def add_group(total_sum, item):
        left, right = item
        partial_value = jnp.dot(left, right, preferred_element_type=jnp.float32)
        rounded = lax.optimization_barrier(partial_value.astype(jnp.bfloat16))
        return (total_sum + rounded.astype(jnp.float32), None)
    summed, unused = lax.scan(add_group, jnp.zeros((TOKENS, D), jnp.float32), (normed_parts, weight_parts))
    return (normed, state_out, summed.astype(jnp.bfloat16))
```

```python
import jax
import jax.numpy as jnp
from jax import lax
from jax.sharding import Mesh, PartitionSpec as P

H = 64
DH = 128
EPSILON = 1e-06
CTX = ("za", "zb", "core")
TP = ("x", "y")
HIGH = lax.Precision.HIGHEST
BF16 = jnp.bfloat16
F32 = jnp.float32


def split3(x):
    hi = lax.reduce_precision(x, 8, 7)
    rest = x - hi
    mid = lax.reduce_precision(rest, 8, 7)
    low = rest - mid
    return jnp.stack([hi.astype(BF16), mid.astype(BF16), low.astype(BF16)])


def join3(parts):
    parts = parts.astype(F32)
    return parts[0] + (parts[1] + parts[2])


def with_rows(block, vector):
    width = block.shape[-1]
    flat = split3(vector).reshape(-1)
    tail = jnp.pad(flat, (0, 16 * width - flat.shape[0])).reshape(16, width)
    lead = block.shape[:-2]
    tail = jnp.broadcast_to(tail, lead + tail.shape)
    return jnp.concatenate([block, tail], axis=-2)


def rows_of(tail, n):
    count = tail.shape[0]
    flat = tail.reshape(count, -1)[:, : 3 * n].reshape(count, 3, n)
    return jnp.sum(join3(jnp.moveaxis(flat, 1, 0)), axis=0)


def per_device(queries, keys, values, log_keep, state_in, norm_gain, out_weight):
    tokens = queries.shape[0]
    heads = log_keep.shape[0]
    parts = lax.axis_size(CTX)
    rows = DH // parts
    nx, ny = lax.axis_size("x"), lax.axis_size("y")

    swap = [(a * nx + b, b * nx + a) for a in range(nx) for b in range(nx)]
    moved = lax.ppermute(out_weight.T, ("za", "x"), swap)
    gathered = lax.all_gather(moved, CTX, axis=0, tiled=True)
    cols = out_weight.shape[1] * parts // (nx * ny)
    gathered = gathered.reshape(nx, ny * cols, out_weight.shape[0])

    q = queries.reshape(tokens, heads, DH)
    k = keys.reshape(tokens, heads, DH)
    v = values.reshape(tokens, heads, DH)
    within = jnp.cumsum(log_keep, axis=1)
    own_log = within[:, -1]
    key_factor = jnp.exp(own_log[:, None] - within).T
    kdec = (k * key_factor[:, :, None]).astype(BF16)
    inc = jnp.einsum("shd,she->hde", kdec, v, preferred_element_type=F32)

    out = inc.astype(BF16).reshape(heads, parts, rows, DH).transpose(1, 0, 2, 3)
    logs = jnp.pad(split3(own_log), ((0, rows - 3), (0, DH - heads)))
    logs = jnp.broadcast_to(logs[None, None], (parts, 1, rows, DH))
    got = lax.all_to_all(jnp.concatenate([out, logs], axis=1), CTX, 0, 0, tiled=True)

    causal = jnp.tril(jnp.ones((tokens, tokens), dtype=bool))
    spread = within[:, :, None] - within[:, None, :]
    decay = jnp.where(causal, jnp.exp(jnp.minimum(spread, 0.0)), 0.0)
    scores = jnp.einsum("shd,thd->hst", q, k, preferred_element_type=F32)
    weights = (scores * decay).astype(BF16)
    intra = jnp.einsum("hst,thd->shd", weights, v, preferred_element_type=F32)

    incs = got[:, :heads].astype(F32)
    every = join3(jnp.moveaxis(got[:, heads, :3, :heads], 1, 0))
    upto = jnp.concatenate([jnp.zeros((1, heads), F32), jnp.cumsum(every, axis=0)])
    order = jnp.arange(parts)
    before = order[None, :] < jnp.arange(parts + 1)[:, None]
    gap = upto[:, None] - upto[None, 1:]
    mixing = jnp.where(before[:, :, None], jnp.exp(jnp.minimum(gap, 0.0)), 0.0)
    me = lax.axis_index(CTX)
    first = lax.dynamic_slice_in_dim(state_in, me * rows, rows, 1)
    states = jnp.einsum("cjh,jhrd->chrd", mixing, incs, precision=HIGH)
    states = states + jnp.exp(upto)[:, :, None, None] * first[None]
    final = states[parts]
    back = lax.all_to_all(states[:parts].astype(BF16), CTX, 0, 0, tiled=True)
    start = back.transpose(1, 0, 2, 3).reshape(heads, DH, DH)

    inter = jnp.einsum("shd,hde->she", q, start, preferred_element_type=F32)
    inter = inter * jnp.exp(within).T[:, :, None]
    attended = (intra + inter).reshape(tokens, heads * DH)
    squares = jnp.sum(attended * attended, axis=1)
    gained = attended * norm_gain

    message = with_rows(gained.astype(BF16), squares)
    message = jnp.broadcast_to(message[None], (nx,) + message.shape)
    acts = lax.all_to_all(message, "x", 0, 0, tiled=True)
    squares = rows_of(acts[:, tokens:], tokens)
    partial = sum(
        lax.dot_general(
            acts[i, :tokens], gathered[i], (((1,), (1,)), ((), ())), preferred_element_type=F32
        )
        for i in range(nx)
    )
    partial = partial.astype(BF16).reshape(tokens, ny, cols).transpose(1, 0, 2)
    shares = lax.all_to_all(with_rows(partial, squares), "y", 0, 0, tiled=True)
    squares = rows_of(shares[:, tokens:], tokens)
    scale = lax.rsqrt(squares / (H * DH) + EPSILON)[:, None]
    normed = (attended * scale * norm_gain).astype(BF16)
    layer_out = (jnp.sum(shares[:, :tokens].astype(F32), axis=0) * scale).astype(BF16)
    return (normed, final, layer_out)


def solution(mesh):
    fine = Mesh(mesh.devices.reshape(4, 4, 2, 4, 4), CTX + TP)
    return jax.shard_map(
        per_device,
        mesh=fine,
        in_specs=(
            P(CTX, TP),
            P(CTX, TP),
            P(CTX, TP),
            P(TP, CTX),
            P(TP, None, None),
            P(TP),
            P(TP, CTX),
        ),
        out_specs=(P(CTX, TP), P(TP, CTX, None), P(CTX, TP)),
        check_vma=False,
    )
```

```python
import jax
import jax.numpy as jnp
from jax import lax
from jax.sharding import Mesh, PartitionSpec as P

H = 64
DH = 128
EPSILON = 1e-06
CTX = ("za", "zb", "core")
INNER = ("zb", "core")
TP = ("x", "y")
HIGH = lax.Precision.HIGHEST
BF16 = jnp.bfloat16
F32 = jnp.float32


def split3(x):
    hi = lax.reduce_precision(x, 8, 7)
    rest = x - hi
    mid = lax.reduce_precision(rest, 8, 7)
    low = rest - mid
    return jnp.stack([hi.astype(BF16), mid.astype(BF16), low.astype(BF16)])


def join3(parts):
    parts = parts.astype(F32)
    return parts[0] + (parts[1] + parts[2])


def with_rows(block, vector):
    width = block.shape[-1]
    flat = split3(vector).reshape(-1)
    tail = jnp.pad(flat, (0, 16 * width - flat.shape[0])).reshape(16, width)
    lead = block.shape[:-2]
    tail = jnp.broadcast_to(tail, lead + tail.shape)
    return jnp.concatenate([block, tail], axis=-2)


def rows_of(tail, n):
    count = tail.shape[0]
    flat = tail.reshape(count, -1)[:, : 3 * n].reshape(count, 3, n)
    return jnp.sum(join3(jnp.moveaxis(flat, 1, 0)), axis=0)


def mixer(logs):
    count, heads = logs.shape
    upto = jnp.concatenate([jnp.zeros((1, heads), F32), jnp.cumsum(logs, axis=0)])
    before = jnp.arange(count)[None, :] < jnp.arange(count + 1)[:, None]
    gap = upto[:, None] - upto[None, 1:]
    factor = jnp.where(before[:, :, None], jnp.exp(jnp.minimum(gap, 0.0)), 0.0)
    return upto, factor


def per_device(queries, keys, values, log_keep, state_in, norm_gain, out_weight):
    tokens = queries.shape[0]
    heads = log_keep.shape[0]
    parts = lax.axis_size(CTX)
    quads, inner = lax.axis_size("za"), lax.axis_size(INNER)
    rows = DH // parts
    slab = heads * quads * rows
    nx, ny = lax.axis_size("x"), lax.axis_size("y")

    swap = [(a * nx + b, b * nx + a) for a in range(nx) for b in range(nx)]
    moved = lax.ppermute(out_weight.T, ("za", "x"), swap)
    gathered = lax.all_gather(moved, CTX, axis=0, tiled=True)
    cols = out_weight.shape[1] * parts // (nx * ny)
    gathered = gathered.reshape(nx, ny * cols, out_weight.shape[0])

    q = queries.reshape(tokens, heads, DH)
    k = keys.reshape(tokens, heads, DH)
    v = values.reshape(tokens, heads, DH)
    within = jnp.cumsum(log_keep, axis=1)
    own_log = within[:, -1]
    key_factor = jnp.exp(own_log[:, None] - within).T
    kdec = (k * key_factor[:, :, None]).astype(BF16)
    inc = jnp.einsum("shd,she->hde", kdec, v, preferred_element_type=F32)

    out = inc.astype(BF16).reshape(heads, quads, inner, rows, DH)
    out = out.transpose(2, 0, 1, 3, 4).reshape(inner, slab, DH)
    logs = jnp.pad(split3(own_log), ((0, 5), (0, DH - heads)))
    logs = jnp.broadcast_to(logs[None], (inner,) + logs.shape)
    got = lax.all_to_all(jnp.concatenate([out, logs], axis=1), INNER, 0, 0, tiled=True)

    causal = jnp.tril(jnp.ones((tokens, tokens), dtype=bool))
    spread = within[:, :, None] - within[:, None, :]
    decay = jnp.where(causal, jnp.exp(jnp.minimum(spread, 0.0)), 0.0)
    scores = jnp.einsum("shd,thd->hst", q, k, preferred_element_type=F32)
    weights = (scores * decay).astype(BF16)
    intra = jnp.einsum("hst,thd->shd", weights, v, preferred_element_type=F32)

    incs = got[:, :slab].astype(F32).reshape(inner, heads, -1)
    upto, mixing = mixer(join3(jnp.moveaxis(got[:, slab : slab + 3, :heads], 1, 0)))
    local = jnp.einsum("cjh,jhn->chn", mixing, incs, precision=HIGH)

    total_log = jnp.pad(upto[inner], (0, DH - heads))
    total_log = jnp.pad(total_log[None], ((0, 7), (0, 0)))
    total = jnp.concatenate([local[inner].reshape(slab, DH), total_log])
    totals = lax.all_to_all(
        jnp.broadcast_to(total[None], (quads,) + total.shape), "za", 0, 0, tiled=True
    )
    after, across = mixer(totals[:, slab, :heads])
    first = lax.dynamic_index_in_dim(
        state_in.reshape(heads, quads, inner, rows, DH), lax.axis_index(INNER), 2, keepdims=False
    ).reshape(heads, -1)
    bounds = jnp.einsum(
        "cjh,jhn->chn", across, totals[:, :slab].reshape(quads, heads, -1), precision=HIGH
    )
    bounds = bounds + jnp.exp(after)[:, :, None] * first[None]
    quad = lax.axis_index("za")
    final = lax.dynamic_index_in_dim(
        bounds[quads].reshape(heads, quads, rows, DH), quad, 1, keepdims=False
    )
    opening = lax.dynamic_index_in_dim(bounds, quad, 0, keepdims=False)
    states = local[:inner] + jnp.exp(upto[:inner])[:, :, None] * opening[None]
    states = states.astype(BF16).reshape(inner, slab, DH)
    back = lax.all_to_all(states, INNER, 0, 0, tiled=True)
    start = back.reshape(inner, heads, quads, rows, DH).transpose(1, 2, 0, 3, 4)
    start = start.reshape(heads, DH, DH)

    inter = jnp.einsum("shd,hde->she", q, start, preferred_element_type=F32)
    inter = inter * jnp.exp(within).T[:, :, None]
    attended = (intra + inter).reshape(tokens, heads * DH)
    squares = jnp.sum(attended * attended, axis=1)
    gained = attended * norm_gain

    message = with_rows(gained.astype(BF16), squares)
    message = jnp.broadcast_to(message[None], (nx,) + message.shape)
    acts = lax.all_to_all(message, "x", 0, 0, tiled=True)
    squares = rows_of(acts[:, tokens:], tokens)
    partial = sum(
        lax.dot_general(
            acts[i, :tokens], gathered[i], (((1,), (1,)), ((), ())), preferred_element_type=F32
        )
        for i in range(nx)
    )
    partial = partial.astype(BF16).reshape(tokens, ny, cols).transpose(1, 0, 2)
    shares = lax.all_to_all(with_rows(partial, squares), "y", 0, 0, tiled=True)
    squares = rows_of(shares[:, tokens:], tokens)
    scale = lax.rsqrt(squares / (H * DH) + EPSILON)[:, None]
    normed = (attended * scale * norm_gain).astype(BF16)
    layer_out = (jnp.sum(shares[:, :tokens].astype(F32), axis=0) * scale).astype(BF16)
    return (normed, final, layer_out)


def solution(mesh):
    fine = Mesh(mesh.devices.reshape(4, 4, 2, 4, 4), CTX + TP)
    return jax.shard_map(
        per_device,
        mesh=fine,
        in_specs=(
            P(CTX, TP),
            P(CTX, TP),
            P(CTX, TP),
            P(TP, CTX),
            P(TP, None, None),
            P(TP),
            P(TP, CTX),
        ),
        out_specs=(P(CTX, TP), P(TP, CTX, None), P(CTX, TP)),
        check_vma=False,
    )
```

```python
import jax
import jax.numpy as jnp
from jax import lax
from jax.sharding import Mesh, PartitionSpec as P

H = 64
DH = 128
EPSILON = 1e-06
CTX = ("za", "zb", "core")
INNER = ("zb", "core")
TP = ("x", "y")
HIGH = lax.Precision.HIGHEST
BF16 = jnp.bfloat16
F32 = jnp.float32


def split3(x):
    hi = lax.reduce_precision(x, 8, 7)
    rest = x - hi
    mid = lax.reduce_precision(rest, 8, 7)
    low = rest - mid
    return jnp.stack([hi.astype(BF16), mid.astype(BF16), low.astype(BF16)])


def join3(parts):
    parts = parts.astype(F32)
    return parts[0] + (parts[1] + parts[2])


def with_rows(block, vector):
    width = block.shape[-1]
    flat = split3(vector).reshape(-1)
    tail = jnp.pad(flat, (0, 16 * width - flat.shape[0])).reshape(16, width)
    lead = block.shape[:-2]
    tail = jnp.broadcast_to(tail, lead + tail.shape)
    return jnp.concatenate([block, tail], axis=-2)


def rows_of(tail, n):
    count = tail.shape[0]
    flat = tail.reshape(count, -1)[:, : 3 * n].reshape(count, 3, n)
    return jnp.sum(join3(jnp.moveaxis(flat, 1, 0)), axis=0)


def mixer(logs):
    count, heads = logs.shape
    upto = jnp.concatenate([jnp.zeros((1, heads), F32), jnp.cumsum(logs, axis=0)])
    before = jnp.arange(count)[None, :] < jnp.arange(count + 1)[:, None]
    gap = upto[:, None] - upto[None, 1:]
    factor = jnp.where(before[:, :, None], jnp.exp(jnp.minimum(gap, 0.0)), 0.0)
    return upto, factor


def per_device(queries, keys, values, log_keep, state_in, norm_gain, out_weight):
    tokens = queries.shape[0]
    heads = log_keep.shape[0]
    parts = lax.axis_size(CTX)
    quads, inner = lax.axis_size("za"), lax.axis_size(INNER)
    rows = DH // parts
    slab = heads * quads * rows
    nx, ny = lax.axis_size("x"), lax.axis_size("y")

    swap = [(a * ny + b, b * ny + a) for a in range(ny) for b in range(ny)]
    moved = lax.ppermute(out_weight.T, ("zb", "y"), swap)
    gathered = lax.all_gather(moved, CTX, axis=0, tiled=True)
    cols = out_weight.shape[1] * parts // (nx * ny)
    gathered = gathered.reshape(nx, ny, cols, out_weight.shape[0])

    q = queries.reshape(tokens, heads, DH)
    k = keys.reshape(tokens, heads, DH)
    v = values.reshape(tokens, heads, DH)
    within = jnp.cumsum(log_keep, axis=1)
    own_log = within[:, -1]
    key_factor = jnp.exp(own_log[:, None] - within).T
    kdec = (k * key_factor[:, :, None]).astype(BF16)
    inc = jnp.einsum("shd,she->hde", kdec, v, preferred_element_type=F32)

    out = inc.astype(BF16).reshape(heads, quads, inner, rows, DH)
    out = out.transpose(2, 0, 1, 3, 4).reshape(inner, slab, DH)
    logs = jnp.pad(split3(own_log), ((0, 5), (0, DH - heads)))
    logs = jnp.broadcast_to(logs[None], (inner,) + logs.shape)
    got = lax.all_to_all(jnp.concatenate([out, logs], axis=1), INNER, 0, 0, tiled=True)

    causal = jnp.tril(jnp.ones((tokens, tokens), dtype=bool))
    spread = within[:, :, None] - within[:, None, :]
    decay = jnp.where(causal, jnp.exp(jnp.minimum(spread, 0.0)), 0.0)
    scores = jnp.einsum("shd,thd->hst", q, k, preferred_element_type=F32)
    weights = (scores * decay).astype(BF16)
    intra = jnp.einsum("hst,thd->shd", weights, v, preferred_element_type=F32)

    incs = got[:, :slab].astype(F32).reshape(inner, heads, -1)
    upto, mixing = mixer(join3(jnp.moveaxis(got[:, slab : slab + 3, :heads], 1, 0)))
    local = jnp.einsum("cjh,jhn->chn", mixing, incs, precision=HIGH)

    total_log = jnp.pad(upto[inner], (0, DH - heads))
    total_log = jnp.pad(total_log[None], ((0, 7), (0, 0)))
    total = jnp.concatenate([local[inner].reshape(slab, DH), total_log])
    totals = lax.all_to_all(
        jnp.broadcast_to(total[None], (quads,) + total.shape), "za", 0, 0, tiled=True
    )
    after, across = mixer(totals[:, slab, :heads])
    first = lax.dynamic_index_in_dim(
        state_in.reshape(heads, quads, inner, rows, DH), lax.axis_index(INNER), 2, keepdims=False
    ).reshape(heads, -1)
    bounds = jnp.einsum(
        "cjh,jhn->chn", across, totals[:, :slab].reshape(quads, heads, -1), precision=HIGH
    )
    bounds = bounds + jnp.exp(after)[:, :, None] * first[None]
    quad = lax.axis_index("za")
    final = lax.dynamic_index_in_dim(
        bounds[quads].reshape(heads, quads, rows, DH), quad, 1, keepdims=False
    )
    opening = lax.dynamic_index_in_dim(bounds, quad, 0, keepdims=False)
    states = local[:inner] + jnp.exp(upto[:inner])[:, :, None] * opening[None]
    states = states.astype(BF16).reshape(inner, slab, DH)
    back = lax.all_to_all(states, INNER, 0, 0, tiled=True)
    start = back.reshape(inner, heads, quads, rows, DH).transpose(1, 2, 0, 3, 4)
    start = start.reshape(heads, DH, DH)

    inter = jnp.einsum("shd,hde->she", q, start, preferred_element_type=F32)
    inter = inter * jnp.exp(within).T[:, :, None]
    attended = (intra + inter).reshape(tokens, heads * DH)
    squares = jnp.sum(attended * attended, axis=1)
    gained = attended * norm_gain

    message = with_rows(gained.astype(BF16), squares)
    message = jnp.broadcast_to(message[None], (ny,) + message.shape)
    acts = lax.all_to_all(message, "y", 0, 0, tiled=True)
    squares = rows_of(acts[:, tokens:], tokens)
    partial = jnp.stack([sum(
        lax.dot_general(
            acts[i, :tokens], gathered[j, i], (((1,), (1,)), ((), ())), preferred_element_type=F32
        )
        for i in range(ny)
    ).astype(BF16) for j in range(nx)])
    shares = lax.all_to_all(with_rows(partial, squares), "x", 0, 0, tiled=True)
    squares = rows_of(shares[:, tokens:], tokens)
    scale = lax.rsqrt(squares / (H * DH) + EPSILON)[:, None]
    normed = (attended * scale * norm_gain).astype(BF16)
    layer_out = (jnp.sum(shares[:, :tokens].astype(F32), axis=0) * scale).astype(BF16)
    return (normed, final, layer_out)


def solution(mesh):
    fine = Mesh(mesh.devices.reshape(4, 4, 2, 4, 4), CTX + TP)
    return jax.shard_map(
        per_device,
        mesh=fine,
        in_specs=(
            P(CTX, TP),
            P(CTX, TP),
            P(CTX, TP),
            P(TP, CTX),
            P(TP, None, None),
            P(TP),
            P(TP, CTX),
        ),
        out_specs=(P(CTX, TP), P(TP, CTX, None), P(CTX, TP)),
        check_vma=False,
    )
```

```python
import jax
import jax.numpy as jnp
from jax import lax
from jax.experimental import pallas as pl
from jax.experimental.pallas import tpu as pltpu
from jax.sharding import Mesh, PartitionSpec as P

H = 64
DH = 128
EPSILON = 1e-06
CTX = ("za", "zb", "core")
INNER = ("zb", "core")
TP = ("x", "y")
HIGH = lax.Precision.HIGHEST
BF16 = jnp.bfloat16
F32 = jnp.float32


def split3(x):
    hi = lax.reduce_precision(x, 8, 7)
    rest = x - hi
    mid = lax.reduce_precision(rest, 8, 7)
    low = rest - mid
    return jnp.stack([hi.astype(BF16), mid.astype(BF16), low.astype(BF16)])


def join3(parts):
    parts = parts.astype(F32)
    return parts[0] + (parts[1] + parts[2])


def tail_of(vector, width):
    flat = split3(vector).reshape(-1)
    return jnp.pad(flat, (0, 16 * width - flat.shape[0])).reshape(16, width)


def rows_of(tail, n):
    count = tail.shape[0]
    flat = tail.reshape(count, -1)[:, : 3 * n].reshape(count, 3, n)
    return jnp.sum(join3(jnp.moveaxis(flat, 1, 0)), axis=0)


def mixer(logs):
    count, heads = logs.shape
    upto = jnp.concatenate([jnp.zeros((1, heads), F32), jnp.cumsum(logs, axis=0)])
    before = jnp.arange(count)[None, :] < jnp.arange(count + 1)[:, None]
    gap = upto[:, None] - upto[None, 1:]
    factor = jnp.where(before[:, :, None], jnp.exp(jnp.minimum(gap, 0.0)), 0.0)
    return upto, factor


def project_kernel(x_ref, acts_ref, weights_ref, tail_ref, *refs):
    outs, total = refs[:-1], refs[-1]
    tokens = total.shape[0]
    block, half = pl.program_id(0), pl.program_id(1)
    depth = weights_ref.shape[1]
    value = sum(
        lax.dot_general(
            acts_ref[half * depth + i, :tokens, :],
            weights_ref[0, i],
            (((1,), (1,)), ((), ())),
            preferred_element_type=F32,
        )
        for i in range(depth)
    )

    @pl.when(half == 0)
    def _():
        total[...] = value

    for j, out in enumerate(outs):
        @pl.when((half == 1) & (block == j))
        def _():
            out[:tokens, :] = (total[...] + value).astype(BF16)
            out[tokens:, :] = tail_ref[...]


def project(acts, weights, tail, x):
    nx, ny, cols, inner = weights.shape
    rows = acts.shape[1]
    return pl.pallas_call(
        project_kernel,
        out_shape=[jax.ShapeDtypeStruct((rows, cols), BF16)] * nx,
        grid_spec=pltpu.PrefetchScalarGridSpec(
            num_scalar_prefetch=1,
            grid=(nx, 2),
            in_specs=[
                pl.BlockSpec(acts.shape, lambda j, h, x: (0, 0, 0)),
                pl.BlockSpec((1, ny // 2, cols, inner), lambda j, h, x: (lax.rem(x[0] + j, nx), h, 0, 0)),
                pl.BlockSpec(tail.shape, lambda j, h, x: (0, 0)),
            ],
            out_specs=[pl.BlockSpec((rows, cols), lambda j, h, x: (0, 0))] * nx,
            scratch_shapes=[pltpu.VMEM((rows - tail.shape[0], cols), F32)],
        ),
        name="project",
    )(x.reshape(1).astype(jnp.int32), acts, weights, tail)


def per_device(queries, keys, values, log_keep, state_in, norm_gain, out_weight):
    tokens = queries.shape[0]
    heads = log_keep.shape[0]
    parts = lax.axis_size(CTX)
    quads, inner = lax.axis_size("za"), lax.axis_size(INNER)
    rows = DH // parts
    slab = heads * quads * rows
    nx, ny = lax.axis_size("x"), lax.axis_size("y")

    swap = [(a * ny + b, b * ny + a) for a in range(ny) for b in range(ny)]
    moved = lax.ppermute(out_weight.T, ("zb", "y"), swap)

    q = queries.reshape(tokens, heads, DH)
    k = keys.reshape(tokens, heads, DH)
    v = values.reshape(tokens, heads, DH)
    within = jnp.cumsum(log_keep, axis=1)
    own_log = within[:, -1]
    key_factor = jnp.exp(own_log[:, None] - within).T
    kdec = (k * key_factor[:, :, None]).astype(BF16)
    inc = jnp.einsum("shd,she->hde", kdec, v, preferred_element_type=F32)

    out = inc.astype(BF16).reshape(heads, quads, inner, rows, DH)
    out = out.transpose(2, 0, 1, 3, 4).reshape(inner, slab, DH)
    logs = jnp.pad(split3(own_log), ((0, 5), (0, DH - heads)))
    logs = jnp.broadcast_to(logs[None], (inner,) + logs.shape)
    opener = jnp.concatenate([out, logs], axis=1)
    got = lax.all_to_all(opener, INNER, 0, 0, tiled=True)

    moved, opener = lax.optimization_barrier((moved, opener))
    gathered = lax.all_gather(moved, CTX, axis=0, tiled=True)
    cols = out_weight.shape[1] * parts // (nx * ny)
    gathered = gathered.reshape(nx, ny, cols, out_weight.shape[0])

    causal = jnp.tril(jnp.ones((tokens, tokens), dtype=bool))
    spread = within[:, :, None] - within[:, None, :]
    decay = jnp.where(causal, jnp.exp(jnp.minimum(spread, 0.0)), 0.0)
    scores = jnp.einsum("shd,thd->hst", q, k, preferred_element_type=F32)
    weights = (scores * decay).astype(BF16)
    intra = jnp.einsum("hst,thd->shd", weights, v, preferred_element_type=F32)

    incs = got[:, :slab].astype(F32).reshape(inner, heads, -1)
    upto, mixing = mixer(join3(jnp.moveaxis(got[:, slab : slab + 3, :heads], 1, 0)))
    local = jnp.einsum("cjh,jhn->chn", mixing, incs, precision=HIGH)

    total_log = jnp.pad(upto[inner], (0, DH - heads))
    total_log = jnp.pad(total_log[None], ((0, 7), (0, 0)))
    total = jnp.concatenate([local[inner].reshape(slab, DH), total_log])
    totals = lax.all_to_all(
        jnp.broadcast_to(total[None], (quads,) + total.shape), "za", 0, 0, tiled=True
    )
    after, across = mixer(totals[:, slab, :heads])
    first = lax.dynamic_index_in_dim(
        state_in.reshape(heads, quads, inner, rows, DH), lax.axis_index(INNER), 2, keepdims=False
    ).reshape(heads, -1)
    bounds = jnp.einsum(
        "cjh,jhn->chn", across, totals[:, :slab].reshape(quads, heads, -1), precision=HIGH
    )
    bounds = bounds + jnp.exp(after)[:, :, None] * first[None]
    quad = lax.axis_index("za")
    final = lax.dynamic_index_in_dim(
        bounds[quads].reshape(heads, quads, rows, DH), quad, 1, keepdims=False
    )
    opening = lax.dynamic_index_in_dim(bounds, quad, 0, keepdims=False)
    states = local[:inner] + jnp.exp(upto[:inner])[:, :, None] * opening[None]
    states = states.astype(BF16).reshape(inner, slab, DH)
    back = lax.all_to_all(states, INNER, 0, 0, tiled=True)
    start = back.reshape(inner, heads, quads, rows, DH).transpose(1, 2, 0, 3, 4)
    start = start.reshape(heads, DH, DH)

    inter = jnp.einsum("shd,hde->she", q, start, preferred_element_type=F32)
    inter = inter * jnp.exp(within).T[:, :, None]
    attended = (intra + inter).reshape(tokens, heads * DH)
    squares = jnp.sum(attended * attended, axis=1)
    gained = attended * norm_gain

    message = jnp.concatenate([gained.astype(BF16), tail_of(squares, heads * DH)])
    message = jnp.broadcast_to(message[None], (ny,) + message.shape)
    acts = lax.all_to_all(message, "y", 0, 0, tiled=True)
    squares = rows_of(acts[:, tokens:], tokens)
    blocks = project(acts, gathered, tail_of(squares, cols), lax.axis_index("x"))
    shares = [blocks[0]]
    for step in (2, 1, 3):
        ring = [(i, (i + step) % nx) for i in range(nx)]
        shares.append(lax.ppermute(blocks[step], "x", ring))
    squares = rows_of(jnp.stack([share[tokens:] for share in shares]), tokens)
    scale = lax.rsqrt(squares / (H * DH) + EPSILON)[:, None]
    normed = (attended * scale * norm_gain).astype(BF16)
    layer_out = (sum(share[:tokens].astype(F32) for share in shares) * scale).astype(BF16)
    return (normed, final, layer_out)


def solution(mesh):
    fine = Mesh(mesh.devices.reshape(4, 4, 2, 4, 4), CTX + TP)
    return jax.shard_map(
        per_device,
        mesh=fine,
        in_specs=(
            P(CTX, TP),
            P(CTX, TP),
            P(CTX, TP),
            P(TP, CTX),
            P(TP, None, None),
            P(TP),
            P(TP, CTX),
        ),
        out_specs=(P(CTX, TP), P(TP, CTX, None), P(CTX, TP)),
        check_vma=False,
    )
```

```python
import functools

import jax
import jax.numpy as jnp
from jax import lax
from jax.experimental import pallas as pl
from jax.experimental.pallas import tpu as pltpu
from jax.sharding import Mesh, PartitionSpec as P

H = 64
DH = 128
EPSILON = 1e-06
CTX = ("za", "zb", "core")
INNER = ("zb", "core")
TP = ("x", "y")
FLIGHT = 6
HIGH = lax.Precision.HIGHEST
BF16 = jnp.bfloat16
F32 = jnp.float32


def split3(x):
    hi = lax.reduce_precision(x, 8, 7)
    rest = x - hi
    mid = lax.reduce_precision(rest, 8, 7)
    low = rest - mid
    return jnp.stack([hi.astype(BF16), mid.astype(BF16), low.astype(BF16)])


def join3(parts):
    parts = parts.astype(F32)
    return parts[0] + (parts[1] + parts[2])


def tail_of(vector, width):
    flat = split3(vector).reshape(-1)
    return jnp.pad(flat, (0, 16 * width - flat.shape[0])).reshape(16, width)


def rows_of(tail, n):
    count = tail.shape[0]
    flat = tail.reshape(count, -1)[:, : 3 * n].reshape(count, 3, n)
    return jnp.sum(join3(jnp.moveaxis(flat, 1, 0)), axis=0)


def mixer(logs):
    count, heads = logs.shape
    upto = jnp.concatenate([jnp.zeros((1, heads), F32), jnp.cumsum(logs, axis=0)])
    before = jnp.arange(count)[None, :] < jnp.arange(count + 1)[:, None]
    gap = upto[:, None] - upto[None, 1:]
    factor = jnp.where(before[:, :, None], jnp.exp(jnp.minimum(gap, 0.0)), 0.0)
    return upto, factor


def place_of(z, y, count):
    return lax.rem(z + jnp.where(y == 3, count - 1, y), count)


def project_kernel(targets, at_ref, acts_ref, weights_ref, tail_ref, *refs):
    outs, (left, right, sems) = refs[: len(targets)], refs[len(targets) :]
    tokens = acts_ref.shape[1] - tail_ref.shape[0]
    ny = acts_ref.shape[0]
    x, y = at_ref[0], at_ref[1]
    count = weights_ref.shape[0]
    nx = count // ny
    copies = []
    for n, step in enumerate(targets):
        z = lax.rem(x + step, nx) * ny + y
        for i in range(ny):
            pair = []
            if n == 0:
                pair.append(pltpu.make_async_copy(acts_ref.at[i], left.at[i], sems.at[len(targets), i]))
            source = weights_ref.at[place_of(z, i, count)]
            pair.append(pltpu.make_async_copy(source, right.at[n, i], sems.at[n, i]))
            copies.append(pair)
    for pair in copies[:FLIGHT]:
        for copy in pair:
            copy.start()
    m = 0
    for n, out in enumerate(outs):
        total = None
        for i in range(ny):
            for copy in copies[m]:
                copy.wait()
            if m + FLIGHT < len(copies):
                for copy in copies[m + FLIGHT]:
                    copy.start()
            m += 1
            value = lax.dot_general(
                left[i, :tokens, :],
                right[n, i],
                (((1,), (1,)), ((), ())),
                preferred_element_type=F32,
            )
            total = value if total is None else total + value
        out[:tokens, :] = total.astype(BF16)
        out[tokens:, :] = tail_ref[...]


def project(acts, weights, tail, at, targets):
    ny, rows, depth = acts.shape
    cols = weights.shape[1]
    vmem = pl.BlockSpec(memory_space=pltpu.VMEM)
    return pl.pallas_call(
        functools.partial(project_kernel, targets),
        out_shape=[jax.ShapeDtypeStruct((rows, cols), BF16)] * len(targets),
        grid_spec=pltpu.PrefetchScalarGridSpec(
            num_scalar_prefetch=1,
            grid=(),
            in_specs=[pl.BlockSpec(memory_space=pl.ANY)] * 2 + [vmem],
            out_specs=[vmem] * len(targets),
            scratch_shapes=[
                pltpu.VMEM(acts.shape, BF16),
                pltpu.VMEM((len(targets), ny, cols, depth), BF16),
                pltpu.SemaphoreType.DMA((len(targets) + 1, ny)),
            ],
        ),
        name="project",
    )(at, acts, weights, tail)


def per_device(queries, keys, values, log_keep, state_in, norm_gain, out_weight):
    tokens = queries.shape[0]
    heads = log_keep.shape[0]
    parts = lax.axis_size(CTX)
    quads, inner = lax.axis_size("za"), lax.axis_size(INNER)
    rows = DH // parts
    slab = heads * quads * rows
    nx, ny = lax.axis_size("x"), lax.axis_size("y")

    chips = parts // lax.axis_size("core")
    swap = [
        (z * ny + y, ((z + (y if y < 3 else -1)) % chips) * ny + z % ny)
        for z in range(chips)
        for y in range(ny)
    ]
    moved = lax.ppermute(out_weight.T, ("za", "zb", "y"), swap)

    q = queries.reshape(tokens, heads, DH)
    k = keys.reshape(tokens, heads, DH)
    v = values.reshape(tokens, heads, DH)
    within = jnp.cumsum(log_keep, axis=1)
    own_log = within[:, -1]
    key_factor = jnp.exp(own_log[:, None] - within).T
    kdec = (k * key_factor[:, :, None]).astype(BF16)
    inc = jnp.einsum("shd,she->hde", kdec, v, preferred_element_type=F32)

    out = inc.astype(BF16).reshape(heads, quads, inner, rows, DH)
    out = out.transpose(2, 0, 1, 3, 4).reshape(inner, slab, DH)
    logs = jnp.pad(split3(own_log), ((0, 5), (0, DH - heads)))
    logs = jnp.broadcast_to(logs[None], (inner,) + logs.shape)
    opener = jnp.concatenate([out, logs], axis=1)
    got = lax.all_to_all(opener, INNER, 0, 0, tiled=True)

    moved, opener = lax.optimization_barrier((moved, opener))
    gathered = lax.all_gather(moved, CTX, axis=0, tiled=True)
    cols = out_weight.shape[1] * parts // (nx * ny)
    gathered = gathered.reshape(nx * ny, cols, out_weight.shape[0])

    causal = jnp.tril(jnp.ones((tokens, tokens), dtype=bool))
    spread = within[:, :, None] - within[:, None, :]
    decay = jnp.where(causal, jnp.exp(jnp.minimum(spread, 0.0)), 0.0)
    scores = jnp.einsum("shd,thd->hst", q, k, preferred_element_type=F32)
    weights = (scores * decay).astype(BF16)
    intra = jnp.einsum("hst,thd->shd", weights, v, preferred_element_type=F32)

    incs = got[:, :slab].astype(F32).reshape(inner, heads, -1)
    upto, mixing = mixer(join3(jnp.moveaxis(got[:, slab : slab + 3, :heads], 1, 0)))
    local = jnp.einsum("cjh,jhn->chn", mixing, incs, precision=HIGH)

    total_log = jnp.pad(upto[inner], (0, DH - heads))
    total_log = jnp.pad(total_log[None], ((0, 7), (0, 0)))
    total = jnp.concatenate([local[inner].reshape(slab, DH), total_log])
    totals = lax.all_to_all(
        jnp.broadcast_to(total[None], (quads,) + total.shape), "za", 0, 0, tiled=True
    )
    after, across = mixer(totals[:, slab, :heads])
    first = lax.dynamic_index_in_dim(
        state_in.reshape(heads, quads, inner, rows, DH), lax.axis_index(INNER), 2, keepdims=False
    ).reshape(heads, -1)
    bounds = jnp.einsum(
        "cjh,jhn->chn", across, totals[:, :slab].reshape(quads, heads, -1), precision=HIGH
    )
    bounds = bounds + jnp.exp(after)[:, :, None] * first[None]
    quad = lax.axis_index("za")
    final = lax.dynamic_index_in_dim(
        bounds[quads].reshape(heads, quads, rows, DH), quad, 1, keepdims=False
    )
    opening = lax.dynamic_index_in_dim(bounds, quad, 0, keepdims=False)
    states = local[:inner] + jnp.exp(upto[:inner])[:, :, None] * opening[None]
    states = states.astype(BF16).reshape(inner, slab, DH)
    back = lax.all_to_all(states, INNER, 0, 0, tiled=True)
    start = back.reshape(inner, heads, quads, rows, DH).transpose(1, 2, 0, 3, 4)
    start = start.reshape(heads, DH, DH)

    inter = jnp.einsum("shd,hde->she", q, start, preferred_element_type=F32)
    inter = inter * jnp.exp(within).T[:, :, None]
    attended = (intra + inter).reshape(tokens, heads * DH)
    squares = jnp.sum(attended * attended, axis=1)
    gained = attended * norm_gain

    message = jnp.concatenate([gained.astype(BF16), tail_of(squares, heads * DH)])
    message = jnp.broadcast_to(message[None], (ny,) + message.shape)
    acts = lax.all_to_all(message, "y", 0, 0, tiled=True)
    squares = rows_of(acts[:, tokens:], tokens)
    at = jnp.stack([lax.axis_index("x"), lax.axis_index("y")]).astype(jnp.int32)
    tail = tail_of(squares, cols)
    far = project(acts, gathered, tail, at, (2,))
    near = project(acts, gathered, tail, at, (1, 3, 0))
    shares = [near[2]]
    for step, block in ((2, far[0]), (1, near[0]), (3, near[1])):
        ring = [(i, (i + step) % nx) for i in range(nx)]
        shares.append(lax.ppermute(block, "x", ring))
    squares = rows_of(jnp.stack([share[tokens:] for share in shares]), tokens)
    scale = lax.rsqrt(squares / (H * DH) + EPSILON)[:, None]
    normed = (attended * scale * norm_gain).astype(BF16)
    layer_out = (sum(share[:tokens].astype(F32) for share in shares) * scale).astype(BF16)
    return (normed, final, layer_out)


def solution(mesh):
    fine = Mesh(mesh.devices.reshape(4, 4, 2, 4, 4), CTX + TP)
    return jax.shard_map(
        per_device,
        mesh=fine,
        in_specs=(
            P(CTX, TP),
            P(CTX, TP),
            P(CTX, TP),
            P(TP, CTX),
            P(TP, None, None),
            P(TP),
            P(TP, CTX),
        ),
        out_specs=(P(CTX, TP), P(TP, CTX, None), P(CTX, TP)),
        check_vma=False,
    )
```

```python
import functools

import jax
import jax.numpy as jnp
from jax import lax
from jax.experimental import pallas as pl
from jax.experimental.pallas import tpu as pltpu
from jax.sharding import Mesh, PartitionSpec as P

H = 64
DH = 128
EPSILON = 1e-06
CTX = ("za", "zb", "core")
INNER = ("zb", "core")
TP = ("x", "y")
FLIGHT = 6
HIGH = lax.Precision.HIGHEST
BF16 = jnp.bfloat16
F32 = jnp.float32


def split3(x):
    hi = lax.reduce_precision(x, 8, 7)
    rest = x - hi
    mid = lax.reduce_precision(rest, 8, 7)
    low = rest - mid
    return jnp.stack([hi.astype(BF16), mid.astype(BF16), low.astype(BF16)])


def join3(parts):
    parts = parts.astype(F32)
    return parts[0] + (parts[1] + parts[2])


def tail_of(vector, width):
    flat = split3(vector).reshape(-1)
    return jnp.pad(flat, (0, 16 * width - flat.shape[0])).reshape(16, width)


def rows_of(tail, n):
    count = tail.shape[0]
    flat = tail.reshape(count, -1)[:, : 3 * n].reshape(count, 3, n)
    return jnp.sum(join3(jnp.moveaxis(flat, 1, 0)), axis=0)


def mixer(logs):
    count, heads = logs.shape
    upto = jnp.concatenate([jnp.zeros((1, heads), F32), jnp.cumsum(logs, axis=0)])
    before = jnp.arange(count)[None, :] < jnp.arange(count + 1)[:, None]
    gap = upto[:, None] - upto[None, 1:]
    factor = jnp.where(before[:, :, None], jnp.exp(jnp.minimum(gap, 0.0)), 0.0)
    return upto, factor


def z_step(y, core):
    return (0, 1, 2 - 4 * core, -1)[y]


def project_kernel(at_ref, acts_ref, weights_ref, tail_ref, out_ref, left, right, done, sems, out_sems):
    tokens = acts_ref.shape[1] - tail_ref.shape[0]
    ny = acts_ref.shape[0]
    chips, cores, share, _ = weights_ref.shape
    y = at_ref[0]
    copies = []
    for n in range(chips // ny):
        for i in range(ny):
            group = []
            if n == 0:
                group.append(pltpu.make_async_copy(acts_ref.at[i], left.at[i], sems.at[n, i, cores]))
            for c in range(cores):
                z = lax.rem(n * ny + y + chips + z_step(i, c), chips)
                part = right.at[n, i, pl.ds(c * share, share)]
                group.append(pltpu.make_async_copy(weights_ref.at[z, c], part, sems.at[n, i, c]))
            copies.append(group)
    for group in copies[:FLIGHT]:
        for copy in group:
            copy.start()
    m = 0
    leaving = []
    for n in range(chips // ny):
        total = None
        for i in range(ny):
            for copy in copies[m]:
                copy.wait()
            if m + FLIGHT < len(copies):
                for copy in copies[m + FLIGHT]:
                    copy.start()
            m += 1
            value = lax.dot_general(
                left[i, :tokens, :],
                right[n, i],
                (((1,), (1,)), ((), ())),
                preferred_element_type=F32,
            )
            total = value if total is None else total + value
        done[n, :tokens, :] = total.astype(BF16)
        done[n, tokens:, :] = tail_ref[...]
        leaving.append(pltpu.make_async_copy(done.at[n], out_ref.at[n], out_sems.at[n]))
        leaving[-1].start()
    for copy in leaving:
        copy.wait()


def project(acts, weights, tail, at):
    ny, rows, depth = acts.shape
    chips, cores, share, _ = weights.shape
    nx, cols = chips // ny, cores * share
    hbm = pl.BlockSpec(memory_space=pl.ANY)
    return pl.pallas_call(
        project_kernel,
        out_shape=jax.ShapeDtypeStruct((nx, rows, cols), BF16),
        grid_spec=pltpu.PrefetchScalarGridSpec(
            num_scalar_prefetch=1,
            grid=(),
            in_specs=[hbm, hbm, pl.BlockSpec(memory_space=pltpu.VMEM)],
            out_specs=hbm,
            scratch_shapes=[
                pltpu.VMEM(acts.shape, BF16),
                pltpu.VMEM((nx, ny, cols, depth), BF16),
                pltpu.VMEM((nx, rows, cols), BF16),
                pltpu.SemaphoreType.DMA((nx, ny, cores + 1)),
                pltpu.SemaphoreType.DMA((nx,)),
            ],
        ),
        name="project",
    )(at, acts, weights, tail)


def open_kernel(quads, keep_ref, keys_ref, values_ref, message_ref, across_ref, down_ref):
    tokens = keys_ref.shape[0]
    heads = keep_ref.shape[0]
    inner = message_ref.shape[0]
    each = DH // inner
    step = each // quads
    row = lax.broadcasted_iota(jnp.int32, (tokens, tokens), 0)
    col = lax.broadcasted_iota(jnp.int32, (tokens, tokens), 1)
    sums = (col <= row).astype(F32)
    keep = keep_ref[...]
    down = lax.dot_general(sums, keep, (((1,), (1,)), ((), ())), precision=HIGH, preferred_element_type=F32)
    across_ref[...] = lax.dot_general(
        keep, sums, (((1,), (1,)), ((), ())), precision=HIGH, preferred_element_type=F32
    )
    down_ref[...] = down
    last = down[tokens - 1 :, :]
    factor = jnp.exp(last - down)
    to = lax.broadcasted_iota(jnp.int32, (DH, DH), 0)
    of = lax.broadcasted_iota(jnp.int32, (DH, DH), 1)
    wanted = (to % each) // step * (inner * step) + to // each * step + to % step
    order = (of == wanted).astype(BF16)
    for h in range(heads):
        span = slice(h * DH, (h + 1) * DH)
        decayed = (keys_ref[:, span].astype(F32) * factor[:, h : h + 1]).astype(BF16)
        inc = lax.dot_general(
            decayed, values_ref[:, span], (((0,), (0,)), ((), ())), preferred_element_type=F32
        )
        inc = jnp.dot(order, inc.astype(BF16), preferred_element_type=F32).astype(BF16)
        for i in range(inner):
            message_ref[i, h * each : (h + 1) * each, :] = inc[i * each : (i + 1) * each, :]
    lane = lax.broadcasted_iota(jnp.int32, (8, DH), 1)
    line = lax.broadcasted_iota(jnp.int32, (8, DH), 0)
    logs = jnp.zeros((8, DH), F32)
    for h in range(heads):
        logs = jnp.where(lane == h, last[:, h : h + 1], logs)
    hi = logs.astype(BF16).astype(F32)
    mid = (logs - hi).astype(BF16).astype(F32)
    low = logs - hi - mid
    logs = jnp.where(line == 0, hi, jnp.where(line == 1, mid, jnp.where(line == 2, low, 0.0)))
    for i in range(inner):
        message_ref[i, heads * each :, :] = logs.astype(BF16)


def open_scan(log_keep, keys, values, quads, inner):
    heads, tokens = log_keep.shape
    vmem = pl.BlockSpec(memory_space=pltpu.VMEM)
    return pl.pallas_call(
        functools.partial(open_kernel, quads),
        out_shape=[
            jax.ShapeDtypeStruct((inner, heads * DH // inner + 8, DH), BF16),
            jax.ShapeDtypeStruct((heads, tokens), F32),
            jax.ShapeDtypeStruct((tokens, heads), F32),
        ],
        in_specs=[vmem] * 3,
        out_specs=[vmem] * 3,
        name="open_scan",
    )(log_keep, keys, values)


def per_device(queries, keys, values, log_keep, state_in, norm_gain, out_weight):
    tokens = queries.shape[0]
    heads = log_keep.shape[0]
    parts = lax.axis_size(CTX)
    quads, inner = lax.axis_size("za"), lax.axis_size(INNER)
    rows = DH // parts
    slab = heads * quads * rows
    nx, ny = lax.axis_size("x"), lax.axis_size("y")

    cores = lax.axis_size("core")
    chips = parts // cores
    swap = [
        (
            (z * cores + c) * ny + y,
            ((z + z_step(y, c)) % chips * cores + c) * ny + z % ny,
        )
        for z in range(chips)
        for c in range(cores)
        for y in range(ny)
    ]
    moved = lax.ppermute(out_weight.T, CTX + ("y",), swap)

    q = queries.reshape(tokens, heads, DH)
    k = keys.reshape(tokens, heads, DH)
    v = values.reshape(tokens, heads, DH)
    opener, within, within_down = open_scan(log_keep, keys, values, quads, inner)
    got = lax.all_to_all(opener, INNER, 0, 0, tiled=True)

    moved, opener = lax.optimization_barrier((moved, opener))
    gathered = lax.all_gather(moved, CTX, axis=0, tiled=True)
    cols = out_weight.shape[1] * parts // (nx * ny)
    gathered = gathered.reshape(chips, cores, cols // cores, out_weight.shape[0])

    causal = jnp.tril(jnp.ones((tokens, tokens), dtype=bool))
    spread = within[:, :, None] - within[:, None, :]
    decay = jnp.where(causal, jnp.exp(jnp.minimum(spread, 0.0)), 0.0)
    scores = jnp.einsum("shd,thd->hst", q, k, preferred_element_type=F32)
    weights = (scores * decay).astype(BF16)
    intra = jnp.einsum("hst,thd->shd", weights, v, preferred_element_type=F32)

    incs = got[:, :slab].astype(F32).reshape(inner, heads, -1)
    upto, mixing = mixer(join3(jnp.moveaxis(got[:, slab : slab + 3, :heads], 1, 0)))
    local = jnp.einsum("cjh,jhn->chn", mixing, incs, precision=HIGH)

    total_log = jnp.pad(split3(upto[inner]), ((0, 5), (0, DH - heads)))
    total = jnp.concatenate([local[inner].reshape(slab, DH).astype(BF16), total_log])
    totals = lax.all_to_all(
        jnp.broadcast_to(total[None], (quads,) + total.shape), "za", 0, 0, tiled=True
    ).astype(F32)
    after, across = mixer(join3(jnp.moveaxis(totals[:, slab : slab + 3, :heads], 1, 0)))
    first = lax.dynamic_index_in_dim(
        state_in.reshape(heads, quads, inner, rows, DH), lax.axis_index(INNER), 2, keepdims=False
    ).reshape(heads, -1)
    bounds = jnp.einsum(
        "cjh,jhn->chn", across, totals[:, :slab].reshape(quads, heads, -1), precision=HIGH
    )
    bounds = bounds + jnp.exp(after)[:, :, None] * first[None]
    quad = lax.axis_index("za")
    final = lax.dynamic_index_in_dim(
        bounds[quads].reshape(heads, quads, rows, DH), quad, 1, keepdims=False
    )
    opening = lax.dynamic_index_in_dim(bounds, quad, 0, keepdims=False)
    states = local[:inner] + jnp.exp(upto[:inner])[:, :, None] * opening[None]
    states = states.astype(BF16).reshape(inner, slab, DH)
    back = lax.all_to_all(states, INNER, 0, 0, tiled=True)
    start = back.reshape(inner, heads, quads, rows, DH).transpose(1, 2, 0, 3, 4)
    start = start.reshape(heads, DH, DH)

    inter = jnp.einsum("shd,hde->she", q, start, preferred_element_type=F32)
    inter = inter * jnp.exp(within_down)[:, :, None]
    attended = (intra + inter).reshape(tokens, heads * DH)
    squares = jnp.sum(attended * attended, axis=1)
    gained = attended * norm_gain

    message = jnp.concatenate([gained.astype(BF16), tail_of(squares, heads * DH)])
    message = jnp.broadcast_to(message[None], (ny,) + message.shape)
    acts = lax.all_to_all(message, "y", 0, 0, tiled=True)
    squares = rows_of(acts[:, tokens:], tokens)
    at = lax.axis_index("y").astype(jnp.int32).reshape(1)
    blocks = project(acts, gathered, tail_of(squares, cols), at)
    shares = lax.all_to_all(blocks, "x", 0, 0, tiled=True)
    squares = rows_of(shares[:, tokens:], tokens)
    scale = lax.rsqrt(squares / (H * DH) + EPSILON)[:, None]
    normed = (attended * scale * norm_gain).astype(BF16)
    layer_out = (jnp.sum(shares[:, :tokens].astype(F32), axis=0) * scale).astype(BF16)
    return (normed, final, layer_out)


def solution(mesh):
    fine = Mesh(mesh.devices.reshape(4, 4, 2, 4, 4), CTX + TP)
    return jax.shard_map(
        per_device,
        mesh=fine,
        in_specs=(
            P(CTX, TP),
            P(CTX, TP),
            P(CTX, TP),
            P(TP, CTX),
            P(TP, None, None),
            P(TP),
            P(TP, CTX),
        ),
        out_specs=(P(CTX, TP), P(TP, CTX, None), P(CTX, TP)),
        check_vma=False,
    )
```

```python
import functools

import jax
import jax.numpy as jnp
from jax import lax
from jax.experimental import pallas as pl
from jax.experimental.pallas import tpu as pltpu
from jax.sharding import Mesh, PartitionSpec as P

H = 64
DH = 128
EPSILON = 1e-06
CTX = ("za", "zb", "core")
INNER = ("zb", "core")
TP = ("x", "y")
FLIGHT = 6
HIGH = lax.Precision.HIGHEST
BF16 = jnp.bfloat16
F32 = jnp.float32


def split3(x):
    hi = lax.reduce_precision(x, 8, 7)
    rest = x - hi
    mid = lax.reduce_precision(rest, 8, 7)
    low = rest - mid
    return jnp.stack([hi.astype(BF16), mid.astype(BF16), low.astype(BF16)])


def join3(parts):
    parts = parts.astype(F32)
    return parts[0] + (parts[1] + parts[2])


def tail_of(vector, rows, width):
    flat = split3(vector).reshape(-1)
    return jnp.pad(flat, (0, rows * width - flat.shape[0])).reshape(rows, width)


def rows_of(tail, n):
    count = tail.shape[0]
    flat = tail.reshape(count, -1)[:, : 3 * n].reshape(count, 3, n)
    return jnp.sum(join3(jnp.moveaxis(flat, 1, 0)), axis=0)


def mixer(logs):
    count, heads = logs.shape
    upto = jnp.concatenate([jnp.zeros((1, heads), F32), jnp.cumsum(logs, axis=0)])
    before = jnp.arange(count)[None, :] < jnp.arange(count + 1)[:, None]
    gap = upto[:, None] - upto[None, 1:]
    factor = jnp.where(before[:, :, None], jnp.exp(jnp.minimum(gap, 0.0)), 0.0)
    return upto, factor


def z_step(y, core):
    return (0, 1, 2 - 4 * core, -1)[y]


def project_kernel(at_ref, acts_ref, weights_ref, scale_ref, out_ref, left, right, done, sems, out_sems):
    tokens = scale_ref.shape[0]
    ny = acts_ref.shape[0]
    chips, cores, share, _ = weights_ref.shape
    y = at_ref[0]
    copies = []
    for n in range(chips // ny):
        for i in range(ny):
            group = []
            if n == 0:
                group.append(pltpu.make_async_copy(acts_ref.at[i, pl.ds(0, tokens)], left.at[i], sems.at[n, i, cores]))
            for c in range(cores):
                z = lax.rem(n * ny + y + chips + z_step(i, c), chips)
                part = right.at[n, i, pl.ds(c * share, share)]
                group.append(pltpu.make_async_copy(weights_ref.at[z, c], part, sems.at[n, i, c]))
            copies.append(group)
    for group in copies[:FLIGHT]:
        for copy in group:
            copy.start()
    m = 0
    leaving = []
    for n in range(chips // ny):
        total = None
        for i in range(ny):
            for copy in copies[m]:
                copy.wait()
            if m + FLIGHT < len(copies):
                for copy in copies[m + FLIGHT]:
                    copy.start()
            m += 1
            value = lax.dot_general(
                left[i],
                right[n, i],
                (((1,), (1,)), ((), ())),
                preferred_element_type=F32,
            )
            total = value if total is None else total + value
        done[n] = (total * scale_ref[...]).astype(BF16)
        leaving.append(pltpu.make_async_copy(done.at[n], out_ref.at[n], out_sems.at[n]))
        leaving[-1].start()
    for copy in leaving:
        copy.wait()


def project(acts, weights, scale, at):
    ny, _, depth = acts.shape
    rows = scale.shape[0]
    chips, cores, share, _ = weights.shape
    nx, cols = chips // ny, cores * share
    hbm = pl.BlockSpec(memory_space=pl.ANY)
    return pl.pallas_call(
        project_kernel,
        out_shape=jax.ShapeDtypeStruct((nx, rows, cols), BF16),
        grid_spec=pltpu.PrefetchScalarGridSpec(
            num_scalar_prefetch=1,
            grid=(),
            in_specs=[hbm, hbm, pl.BlockSpec(memory_space=pltpu.VMEM)],
            out_specs=hbm,
            scratch_shapes=[
                pltpu.VMEM((ny, rows, depth), BF16),
                pltpu.VMEM((nx, ny, cols, depth), BF16),
                pltpu.VMEM((nx, rows, cols), BF16),
                pltpu.SemaphoreType.DMA((nx, ny, cores + 1)),
                pltpu.SemaphoreType.DMA((nx,)),
            ],
        ),
        name="project",
    )(at, acts, weights, scale)


def open_kernel(quads, keep_ref, keys_ref, values_ref, message_ref, across_ref, down_ref):
    tokens = keys_ref.shape[0]
    heads = keep_ref.shape[0]
    inner = message_ref.shape[0]
    each = DH // inner
    step = each // quads
    row = lax.broadcasted_iota(jnp.int32, (tokens, tokens), 0)
    col = lax.broadcasted_iota(jnp.int32, (tokens, tokens), 1)
    sums = (col <= row).astype(F32)
    keep = keep_ref[...]
    down = lax.dot_general(sums, keep, (((1,), (1,)), ((), ())), precision=HIGH, preferred_element_type=F32)
    across_ref[...] = lax.dot_general(
        keep, sums, (((1,), (1,)), ((), ())), precision=HIGH, preferred_element_type=F32
    )
    down_ref[...] = down
    last = down[tokens - 1 :, :]
    factor = jnp.exp(last - down)
    to = lax.broadcasted_iota(jnp.int32, (DH, DH), 0)
    of = lax.broadcasted_iota(jnp.int32, (DH, DH), 1)
    wanted = (to % each) // step * (inner * step) + to // each * step + to % step
    order = (of == wanted).astype(BF16)
    for h in range(heads):
        span = slice(h * DH, (h + 1) * DH)
        decayed = (keys_ref[:, span].astype(F32) * factor[:, h : h + 1]).astype(BF16)
        inc = lax.dot_general(
            decayed, values_ref[:, span], (((0,), (0,)), ((), ())), preferred_element_type=F32
        )
        inc = jnp.dot(order, inc.astype(BF16), preferred_element_type=F32).astype(BF16)
        for i in range(inner):
            message_ref[i, h * each : (h + 1) * each, :] = inc[i * each : (i + 1) * each, :]
    lane = lax.broadcasted_iota(jnp.int32, (8, DH), 1)
    line = lax.broadcasted_iota(jnp.int32, (8, DH), 0)
    logs = jnp.zeros((8, DH), F32)
    for h in range(heads):
        logs = jnp.where(lane == h, last[:, h : h + 1], logs)
    hi = logs.astype(BF16).astype(F32)
    mid = (logs - hi).astype(BF16).astype(F32)
    low = logs - hi - mid
    logs = jnp.where(line == 0, hi, jnp.where(line == 1, mid, jnp.where(line == 2, low, 0.0)))
    for i in range(inner):
        message_ref[i, heads * each :, :] = logs.astype(BF16)


def open_scan(log_keep, keys, values, quads, inner):
    heads, tokens = log_keep.shape
    vmem = pl.BlockSpec(memory_space=pltpu.VMEM)
    return pl.pallas_call(
        functools.partial(open_kernel, quads),
        out_shape=[
            jax.ShapeDtypeStruct((inner, heads * DH // inner + 8, DH), BF16),
            jax.ShapeDtypeStruct((heads, tokens), F32),
            jax.ShapeDtypeStruct((tokens, heads), F32),
        ],
        in_specs=[vmem] * 3,
        out_specs=[vmem] * 3,
        name="open_scan",
    )(log_keep, keys, values)


def per_device(queries, keys, values, log_keep, state_in, norm_gain, out_weight):
    tokens = queries.shape[0]
    heads = log_keep.shape[0]
    parts = lax.axis_size(CTX)
    quads, inner = lax.axis_size("za"), lax.axis_size(INNER)
    rows = DH // parts
    slab = heads * quads * rows
    nx, ny = lax.axis_size("x"), lax.axis_size("y")

    cores = lax.axis_size("core")
    chips = parts // cores
    swap = [
        (
            (z * cores + c) * ny + y,
            ((z + z_step(y, c)) % chips * cores + c) * ny + z % ny,
        )
        for z in range(chips)
        for c in range(cores)
        for y in range(ny)
    ]
    moved = lax.ppermute(out_weight.T, CTX + ("y",), swap)

    q = queries.reshape(tokens, heads, DH)
    k = keys.reshape(tokens, heads, DH)
    v = values.reshape(tokens, heads, DH)
    opener, within, within_down = open_scan(log_keep, keys, values, quads, inner)
    got = lax.all_to_all(opener, INNER, 0, 0, tiled=True)

    moved, opener = lax.optimization_barrier((moved, opener))
    gathered = lax.all_gather(moved, CTX, axis=0, tiled=True)
    cols = out_weight.shape[1] * parts // (nx * ny)
    gathered = gathered.reshape(chips, cores, cols // cores, out_weight.shape[0])

    causal = jnp.tril(jnp.ones((tokens, tokens), dtype=bool))
    spread = within[:, :, None] - within[:, None, :]
    decay = jnp.where(causal, jnp.exp(jnp.minimum(spread, 0.0)), 0.0)
    scores = jnp.einsum("shd,thd->hst", q, k, preferred_element_type=F32)
    weights = (scores * decay).astype(BF16)
    intra = jnp.einsum("hst,thd->shd", weights, v, preferred_element_type=F32)

    incs = got[:, :slab].astype(F32).reshape(inner, heads, -1)
    upto, mixing = mixer(join3(jnp.moveaxis(got[:, slab : slab + 3, :heads], 1, 0)))
    local = jnp.einsum("cjh,jhn->chn", mixing, incs, precision=HIGH)

    total_log = jnp.pad(split3(upto[inner]), ((0, 5), (0, DH - heads)))
    total = jnp.concatenate([local[inner].reshape(slab, DH).astype(BF16), total_log])
    totals = lax.all_to_all(
        jnp.broadcast_to(total[None], (quads,) + total.shape), "za", 0, 0, tiled=True
    ).astype(F32)
    after, across = mixer(join3(jnp.moveaxis(totals[:, slab : slab + 3, :heads], 1, 0)))
    first = lax.dynamic_index_in_dim(
        state_in.reshape(heads, quads, inner, rows, DH), lax.axis_index(INNER), 2, keepdims=False
    ).reshape(heads, -1)
    bounds = jnp.einsum(
        "cjh,jhn->chn", across, totals[:, :slab].reshape(quads, heads, -1), precision=HIGH
    )
    bounds = bounds + jnp.exp(after)[:, :, None] * first[None]
    quad = lax.axis_index("za")
    final = lax.dynamic_index_in_dim(
        bounds[quads].reshape(heads, quads, rows, DH), quad, 1, keepdims=False
    )
    opening = lax.dynamic_index_in_dim(bounds, quad, 0, keepdims=False)
    states = local[:inner] + jnp.exp(upto[:inner])[:, :, None] * opening[None]
    states = states.astype(BF16).reshape(inner, slab, DH)
    back = lax.all_to_all(states, INNER, 0, 0, tiled=True)
    start = back.reshape(inner, heads, quads, rows, DH).transpose(1, 2, 0, 3, 4)
    start = start.reshape(heads, DH, DH)

    inter = jnp.einsum("shd,hde->she", q, start, preferred_element_type=F32)
    inter = inter * jnp.exp(within_down)[:, :, None]
    attended = (intra + inter).reshape(tokens, heads * DH)
    squares = jnp.sum(attended * attended, axis=1)
    gained = attended * norm_gain

    message = jnp.concatenate([gained.astype(BF16), tail_of(squares, 16, heads * DH)])
    message = jnp.broadcast_to(message[None], (ny,) + message.shape)
    acts = lax.all_to_all(message, "y", 0, 0, tiled=True)
    squares = rows_of(acts[:, tokens:], tokens)
    mine = tail_of(squares, 8, DH)
    each = lax.all_to_all(jnp.broadcast_to(mine[None], (nx,) + mine.shape), "x", 0, 0, tiled=True)
    scale = lax.rsqrt(rows_of(each, tokens) / (H * DH) + EPSILON)[:, None]
    normed = (attended * scale * norm_gain).astype(BF16)
    at = lax.axis_index("y").astype(jnp.int32).reshape(1)
    shares = lax.all_to_all(project(acts, gathered, scale, at), "x", 0, 0, tiled=True)
    layer_out = jnp.sum(shares.astype(F32), axis=0).astype(BF16)
    return (normed, final, layer_out)


def solution(mesh):
    fine = Mesh(mesh.devices.reshape(4, 4, 2, 4, 4), CTX + TP)
    return jax.shard_map(
        per_device,
        mesh=fine,
        in_specs=(
            P(CTX, TP),
            P(CTX, TP),
            P(CTX, TP),
            P(TP, CTX),
            P(TP, None, None),
            P(TP),
            P(TP, CTX),
        ),
        out_specs=(P(CTX, TP), P(TP, CTX, None), P(CTX, TP)),
        check_vma=False,
    )
```

```python
import functools

import jax
import jax.numpy as jnp
from jax import lax
from jax.experimental import pallas as pl
from jax.experimental.pallas import tpu as pltpu
from jax.sharding import Mesh, PartitionSpec as P

H = 64
DH = 128
EPSILON = 1e-06
CTX = ("za", "zb", "core")
INNER = ("zb", "core")
TP = ("x", "y")
FLIGHT = 6
HIGH = lax.Precision.HIGHEST
BF16 = jnp.bfloat16
F32 = jnp.float32


def split3(x):
    hi = lax.reduce_precision(x, 8, 7)
    rest = x - hi
    mid = lax.reduce_precision(rest, 8, 7)
    low = rest - mid
    return jnp.stack([hi.astype(BF16), mid.astype(BF16), low.astype(BF16)])


def join3(parts):
    parts = parts.astype(F32)
    return parts[0] + (parts[1] + parts[2])


def tail_of(vector, rows, width):
    flat = split3(vector).reshape(-1)
    return jnp.pad(flat, (0, rows * width - flat.shape[0])).reshape(rows, width)


def rows_of(tail, n):
    count = tail.shape[0]
    flat = tail.reshape(count, -1)[:, : 3 * n].reshape(count, 3, n)
    return jnp.sum(join3(jnp.moveaxis(flat, 1, 0)), axis=0)


def mixer(logs):
    count, heads = logs.shape
    upto = jnp.concatenate([jnp.zeros((1, heads), F32), jnp.cumsum(logs, axis=0)])
    before = jnp.arange(count)[None, :] < jnp.arange(count + 1)[:, None]
    gap = upto[:, None] - upto[None, 1:]
    factor = jnp.where(before[:, :, None], jnp.exp(jnp.minimum(gap, 0.0)), 0.0)
    return upto, factor


def z_step(y, core):
    return (0, 1, 2 - 4 * core, -1)[y]


def project_kernel(at_ref, acts_ref, weights_ref, scale_ref, out_ref, right, sems):
    tokens = scale_ref.shape[0]
    ny = acts_ref.shape[0]
    chips, cores, share, _ = weights_ref.shape
    y = at_ref[0]
    copies = []
    for n in range(chips // ny):
        for i in range(ny):
            group = []
            for c in range(cores):
                z = lax.rem(n * ny + y + chips + z_step(i, c), chips)
                part = right.at[n, i, pl.ds(c * share, share)]
                group.append(pltpu.make_async_copy(weights_ref.at[z, c], part, sems.at[n, i, c]))
            copies.append(group)
    for group in copies[:FLIGHT]:
        for copy in group:
            copy.start()
    m = 0
    for n in range(chips // ny):
        total = None
        for i in range(ny):
            for copy in copies[m]:
                copy.wait()
            if m + FLIGHT < len(copies):
                for copy in copies[m + FLIGHT]:
                    copy.start()
            m += 1
            value = lax.dot_general(
                acts_ref[i, :tokens, :],
                right[n, i],
                (((1,), (1,)), ((), ())),
                preferred_element_type=F32,
            )
            total = value if total is None else total + value
        out_ref[n] = (total * scale_ref[...]).astype(BF16)


def project(acts, weights, scale, at):
    ny, _, depth = acts.shape
    rows = scale.shape[0]
    chips, cores, share, _ = weights.shape
    nx, cols = chips // ny, cores * share
    vmem = pl.BlockSpec(memory_space=pltpu.VMEM)
    return pl.pallas_call(
        project_kernel,
        out_shape=pltpu.VMEM((nx, rows, cols), BF16),
        grid_spec=pltpu.PrefetchScalarGridSpec(
            num_scalar_prefetch=1,
            grid=(),
            in_specs=[vmem, pl.BlockSpec(memory_space=pl.ANY), vmem],
            out_specs=vmem,
            scratch_shapes=[
                pltpu.VMEM((nx, ny, cols, depth), BF16),
                pltpu.SemaphoreType.DMA((nx, ny, cores)),
            ],
        ),
        name="project",
    )(at, pltpu.with_memory_space_constraint(acts, pltpu.VMEM), weights, scale)


def open_kernel(quads, keep_ref, keys_ref, values_ref, message_ref, across_ref, down_ref):
    tokens = keys_ref.shape[0]
    heads = keep_ref.shape[0]
    inner = message_ref.shape[0]
    each = DH // inner
    step = each // quads
    row = lax.broadcasted_iota(jnp.int32, (tokens, tokens), 0)
    col = lax.broadcasted_iota(jnp.int32, (tokens, tokens), 1)
    sums = (col <= row).astype(F32)
    keep = keep_ref[...]
    down = lax.dot_general(sums, keep, (((1,), (1,)), ((), ())), precision=HIGH, preferred_element_type=F32)
    across_ref[...] = lax.dot_general(
        keep, sums, (((1,), (1,)), ((), ())), precision=HIGH, preferred_element_type=F32
    )
    down_ref[...] = down
    last = down[tokens - 1 :, :]
    factor = jnp.exp(last - down)
    to = lax.broadcasted_iota(jnp.int32, (DH, DH), 0)
    of = lax.broadcasted_iota(jnp.int32, (DH, DH), 1)
    wanted = (to % each) // step * (inner * step) + to // each * step + to % step
    order = (of == wanted).astype(BF16)
    for h in range(heads):
        span = slice(h * DH, (h + 1) * DH)
        decayed = (keys_ref[:, span].astype(F32) * factor[:, h : h + 1]).astype(BF16)
        inc = lax.dot_general(
            decayed, values_ref[:, span], (((0,), (0,)), ((), ())), preferred_element_type=F32
        )
        inc = jnp.dot(order, inc.astype(BF16), preferred_element_type=F32).astype(BF16)
        for i in range(inner):
            message_ref[i, h * each : (h + 1) * each, :] = inc[i * each : (i + 1) * each, :]
    lane = lax.broadcasted_iota(jnp.int32, (8, DH), 1)
    line = lax.broadcasted_iota(jnp.int32, (8, DH), 0)
    logs = jnp.zeros((8, DH), F32)
    for h in range(heads):
        logs = jnp.where(lane == h, last[:, h : h + 1], logs)
    hi = logs.astype(BF16).astype(F32)
    mid = (logs - hi).astype(BF16).astype(F32)
    low = logs - hi - mid
    logs = jnp.where(line == 0, hi, jnp.where(line == 1, mid, jnp.where(line == 2, low, 0.0)))
    for i in range(inner):
        message_ref[i, heads * each :, :] = logs.astype(BF16)


def open_scan(log_keep, keys, values, quads, inner):
    heads, tokens = log_keep.shape
    vmem = pl.BlockSpec(memory_space=pltpu.VMEM)
    return pl.pallas_call(
        functools.partial(open_kernel, quads),
        out_shape=[
            jax.ShapeDtypeStruct((inner, heads * DH // inner + 8, DH), BF16),
            jax.ShapeDtypeStruct((heads, tokens), F32),
            jax.ShapeDtypeStruct((tokens, heads), F32),
        ],
        in_specs=[vmem] * 3,
        out_specs=[vmem] * 3,
        name="open_scan",
    )(log_keep, keys, values)


def per_device(queries, keys, values, log_keep, state_in, norm_gain, out_weight):
    tokens = queries.shape[0]
    heads = log_keep.shape[0]
    parts = lax.axis_size(CTX)
    quads, inner = lax.axis_size("za"), lax.axis_size(INNER)
    rows = DH // parts
    slab = heads * quads * rows
    nx, ny = lax.axis_size("x"), lax.axis_size("y")

    cores = lax.axis_size("core")
    chips = parts // cores
    swap = [
        (
            (z * cores + c) * ny + y,
            ((z + z_step(y, c)) % chips * cores + c) * ny + z % ny,
        )
        for z in range(chips)
        for c in range(cores)
        for y in range(ny)
    ]
    moved = lax.ppermute(out_weight.T, CTX + ("y",), swap)

    q = queries.reshape(tokens, heads, DH)
    k = keys.reshape(tokens, heads, DH)
    v = values.reshape(tokens, heads, DH)
    opener, within, within_down = open_scan(log_keep, keys, values, quads, inner)
    got = lax.all_to_all(opener, INNER, 0, 0, tiled=True)

    moved, opener = lax.optimization_barrier((moved, opener))
    gathered = lax.all_gather(moved, CTX, axis=0, tiled=True)
    cols = out_weight.shape[1] * parts // (nx * ny)
    gathered = gathered.reshape(chips, cores, cols // cores, out_weight.shape[0])

    causal = jnp.tril(jnp.ones((tokens, tokens), dtype=bool))
    spread = within[:, :, None] - within[:, None, :]
    decay = jnp.where(causal, jnp.exp(jnp.minimum(spread, 0.0)), 0.0)
    scores = jnp.einsum("shd,thd->hst", q, k, preferred_element_type=F32)
    weights = (scores * decay).astype(BF16)
    intra = jnp.einsum("hst,thd->shd", weights, v, preferred_element_type=F32)

    incs = got[:, :slab].astype(F32).reshape(inner, heads, -1)
    upto, mixing = mixer(join3(jnp.moveaxis(got[:, slab : slab + 3, :heads], 1, 0)))
    local = jnp.einsum("cjh,jhn->chn", mixing, incs, precision=HIGH)

    total_log = jnp.pad(split3(upto[inner]), ((0, 5), (0, DH - heads)))
    total = jnp.concatenate([local[inner].reshape(slab, DH).astype(BF16), total_log])
    totals = lax.all_to_all(
        jnp.broadcast_to(total[None], (quads,) + total.shape), "za", 0, 0, tiled=True
    ).astype(F32)
    after, across = mixer(join3(jnp.moveaxis(totals[:, slab : slab + 3, :heads], 1, 0)))
    first = lax.dynamic_index_in_dim(
        state_in.reshape(heads, quads, inner, rows, DH), lax.axis_index(INNER), 2, keepdims=False
    ).reshape(heads, -1)
    bounds = jnp.einsum(
        "cjh,jhn->chn", across, totals[:, :slab].reshape(quads, heads, -1), precision=HIGH
    )
    bounds = bounds + jnp.exp(after)[:, :, None] * first[None]
    quad = lax.axis_index("za")
    final = lax.dynamic_index_in_dim(
        bounds[quads].reshape(heads, quads, rows, DH), quad, 1, keepdims=False
    )
    opening = lax.dynamic_index_in_dim(bounds, quad, 0, keepdims=False)
    states = local[:inner] + jnp.exp(upto[:inner])[:, :, None] * opening[None]
    states = states.astype(BF16).reshape(inner, slab, DH)
    back = lax.all_to_all(states, INNER, 0, 0, tiled=True)
    start = back.reshape(inner, heads, quads, rows, DH).transpose(1, 2, 0, 3, 4)
    start = start.reshape(heads, DH, DH)

    inter = jnp.einsum("shd,hde->she", q, start, preferred_element_type=F32)
    inter = inter * jnp.exp(within_down)[:, :, None]
    attended = (intra + inter).reshape(tokens, heads * DH)
    squares = jnp.sum(attended * attended, axis=1)
    gained = attended * norm_gain

    message = jnp.concatenate([gained.astype(BF16), tail_of(squares, 16, heads * DH)])
    message = jnp.broadcast_to(message[None], (ny,) + message.shape)
    acts = lax.all_to_all(message, "y", 0, 0, tiled=True)
    squares = rows_of(acts[:, tokens:], tokens)
    mine = tail_of(squares, 8, DH)
    each = lax.all_to_all(jnp.broadcast_to(mine[None], (nx,) + mine.shape), "x", 0, 0, tiled=True)
    scale = lax.rsqrt(rows_of(each, tokens) / (H * DH) + EPSILON)[:, None]
    normed = (attended * scale * norm_gain).astype(BF16)
    at = lax.axis_index("y").astype(jnp.int32).reshape(1)
    shares = lax.all_to_all(project(acts, gathered, scale, at), "x", 0, 0, tiled=True)
    layer_out = jnp.sum(shares.astype(F32), axis=0).astype(BF16)
    return (normed, final, layer_out)


def solution(mesh):
    fine = Mesh(mesh.devices.reshape(4, 4, 2, 4, 4), CTX + TP)
    return jax.shard_map(
        per_device,
        mesh=fine,
        in_specs=(
            P(CTX, TP),
            P(CTX, TP),
            P(CTX, TP),
            P(TP, CTX),
            P(TP, None, None),
            P(TP),
            P(TP, CTX),
        ),
        out_specs=(P(CTX, TP), P(TP, CTX, None), P(CTX, TP)),
        check_vma=False,
    )
```

```python
import functools

import jax
import jax.numpy as jnp
from jax import lax
from jax.experimental import pallas as pl
from jax.experimental.pallas import tpu as pltpu
from jax.sharding import Mesh, PartitionSpec as P

H = 64
DH = 128
EPSILON = 1e-06
CTX = ("za", "zb", "core")
INNER = ("zb", "core")
TP = ("x", "y")
FLIGHT = 6
HIGH = lax.Precision.HIGHEST
BF16 = jnp.bfloat16
F32 = jnp.float32


def split3(x):
    hi = lax.reduce_precision(x, 8, 7)
    rest = x - hi
    mid = lax.reduce_precision(rest, 8, 7)
    low = rest - mid
    return jnp.stack([hi.astype(BF16), mid.astype(BF16), low.astype(BF16)])


def join3(parts):
    parts = parts.astype(F32)
    return parts[0] + (parts[1] + parts[2])


def tail_of(vector, rows, width):
    flat = split3(vector).reshape(-1)
    return jnp.pad(flat, (0, rows * width - flat.shape[0])).reshape(rows, width)


def rows_of(tail, n):
    count = tail.shape[0]
    flat = tail.reshape(count, -1)[:, : 3 * n].reshape(count, 3, n)
    return jnp.sum(join3(jnp.moveaxis(flat, 1, 0)), axis=0)


def mixer(logs):
    count, heads = logs.shape
    upto = jnp.concatenate([jnp.zeros((1, heads), F32), jnp.cumsum(logs, axis=0)])
    before = jnp.arange(count)[None, :] < jnp.arange(count + 1)[:, None]
    gap = upto[:, None] - upto[None, 1:]
    factor = jnp.where(before[:, :, None], jnp.exp(jnp.minimum(gap, 0.0)), 0.0)
    return upto, factor


def z_step(y, core):
    return (0, 1, 2 - 4 * core, -1)[y]


def project_kernel(at_ref, acts_ref, weights_ref, scale_ref, out_ref, right, sems):
    tokens = scale_ref.shape[1]
    ny = acts_ref.shape[0]
    chips, cores, share, _ = weights_ref.shape
    y = at_ref[0]
    copies = []
    for n in range(chips // ny):
        for i in range(ny):
            group = []
            for c in range(cores):
                z = lax.rem(n * ny + y + chips + z_step(i, c), chips)
                part = right.at[n, i, pl.ds(c * share, share)]
                group.append(pltpu.make_async_copy(weights_ref.at[z, c], part, sems.at[n, i, c]))
            copies.append(group)
    for group in copies[:FLIGHT]:
        for copy in group:
            copy.start()
    scale = lax.dot_general(
        scale_ref[...],
        jnp.ones((1, out_ref.shape[2]), F32),
        (((0,), (0,)), ((), ())),
        precision=HIGH,
        preferred_element_type=F32,
    )
    m = 0
    for n in range(chips // ny):
        total = None
        for i in range(ny):
            for copy in copies[m]:
                copy.wait()
            if m + FLIGHT < len(copies):
                for copy in copies[m + FLIGHT]:
                    copy.start()
            m += 1
            value = lax.dot_general(
                acts_ref[i, :tokens, :],
                right[n, i],
                (((1,), (1,)), ((), ())),
                preferred_element_type=F32,
            )
            total = value if total is None else total + value
        out_ref[n] = (total * scale).astype(BF16)


def project(acts, weights, scale, at):
    ny, _, depth = acts.shape
    rows = scale.shape[1]
    chips, cores, share, _ = weights.shape
    nx, cols = chips // ny, cores * share
    vmem = pl.BlockSpec(memory_space=pltpu.VMEM)
    return pl.pallas_call(
        project_kernel,
        out_shape=pltpu.VMEM((nx, rows, cols), BF16),
        grid_spec=pltpu.PrefetchScalarGridSpec(
            num_scalar_prefetch=1,
            grid=(),
            in_specs=[vmem, pl.BlockSpec(memory_space=pl.ANY), vmem],
            out_specs=vmem,
            scratch_shapes=[
                pltpu.VMEM((nx, ny, cols, depth), BF16),
                pltpu.SemaphoreType.DMA((nx, ny, cores)),
            ],
        ),
        name="project",
    )(at, pltpu.with_memory_space_constraint(acts, pltpu.VMEM), weights, scale)


def open_kernel(quads, keep_ref, keys_ref, values_ref, message_ref, across_ref, down_ref):
    tokens = keys_ref.shape[0]
    heads = keep_ref.shape[0]
    inner = message_ref.shape[0]
    each = DH // inner
    step = each // quads
    row = lax.broadcasted_iota(jnp.int32, (tokens, tokens), 0)
    col = lax.broadcasted_iota(jnp.int32, (tokens, tokens), 1)
    sums = (col <= row).astype(F32)
    keep = keep_ref[...]
    down = lax.dot_general(sums, keep, (((1,), (1,)), ((), ())), precision=HIGH, preferred_element_type=F32)
    across_ref[...] = lax.dot_general(
        keep, sums, (((1,), (1,)), ((), ())), precision=HIGH, preferred_element_type=F32
    )
    down_ref[...] = down
    last = down[tokens - 1 :, :]
    factor = jnp.exp(last - down)
    to = lax.broadcasted_iota(jnp.int32, (DH, DH), 0)
    of = lax.broadcasted_iota(jnp.int32, (DH, DH), 1)
    wanted = (to % each) // step * (inner * step) + to // each * step + to % step
    order = (of == wanted).astype(BF16)
    for h in range(heads):
        span = slice(h * DH, (h + 1) * DH)
        decayed = (keys_ref[:, span].astype(F32) * factor[:, h : h + 1]).astype(BF16)
        inc = lax.dot_general(
            decayed, values_ref[:, span], (((0,), (0,)), ((), ())), preferred_element_type=F32
        )
        inc = jnp.dot(order, inc.astype(BF16), preferred_element_type=F32).astype(BF16)
        for i in range(inner):
            message_ref[i, h * each : (h + 1) * each, :] = inc[i * each : (i + 1) * each, :]
    lane = lax.broadcasted_iota(jnp.int32, (8, DH), 1)
    line = lax.broadcasted_iota(jnp.int32, (8, DH), 0)
    logs = jnp.zeros((8, DH), F32)
    for h in range(heads):
        logs = jnp.where(lane == h, last[:, h : h + 1], logs)
    hi = logs.astype(BF16).astype(F32)
    mid = (logs - hi).astype(BF16).astype(F32)
    low = logs - hi - mid
    logs = jnp.where(line == 0, hi, jnp.where(line == 1, mid, jnp.where(line == 2, low, 0.0)))
    for i in range(inner):
        message_ref[i, heads * each :, :] = logs.astype(BF16)


def open_scan(log_keep, keys, values, quads, inner):
    heads, tokens = log_keep.shape
    vmem = pl.BlockSpec(memory_space=pltpu.VMEM)
    return pl.pallas_call(
        functools.partial(open_kernel, quads),
        out_shape=[
            jax.ShapeDtypeStruct((inner, heads * DH // inner + 8, DH), BF16),
            jax.ShapeDtypeStruct((heads, tokens), F32),
            jax.ShapeDtypeStruct((tokens, heads), F32),
        ],
        in_specs=[vmem] * 3,
        out_specs=[vmem] * 3,
        name="open_scan",
    )(log_keep, keys, values)


def per_device(queries, keys, values, log_keep, state_in, norm_gain, out_weight):
    tokens = queries.shape[0]
    heads = log_keep.shape[0]
    parts = lax.axis_size(CTX)
    quads, inner = lax.axis_size("za"), lax.axis_size(INNER)
    rows = DH // parts
    slab = heads * quads * rows
    nx, ny = lax.axis_size("x"), lax.axis_size("y")

    cores = lax.axis_size("core")
    chips = parts // cores
    swap = [
        (
            (z * cores + c) * ny + y,
            ((z + z_step(y, c)) % chips * cores + c) * ny + z % ny,
        )
        for z in range(chips)
        for c in range(cores)
        for y in range(ny)
    ]
    moved = lax.ppermute(out_weight.T, CTX + ("y",), swap)

    q = queries.reshape(tokens, heads, DH)
    k = keys.reshape(tokens, heads, DH)
    v = values.reshape(tokens, heads, DH)
    opener, within, within_down = open_scan(log_keep, keys, values, quads, inner)
    got = lax.all_to_all(opener, INNER, 0, 0, tiled=True)

    moved, opener = lax.optimization_barrier((moved, opener))
    gathered = lax.all_gather(moved, CTX, axis=0, tiled=True)
    cols = out_weight.shape[1] * parts // (nx * ny)
    gathered = gathered.reshape(chips, cores, cols // cores, out_weight.shape[0])

    causal = jnp.tril(jnp.ones((tokens, tokens), dtype=bool))
    spread = within[:, :, None] - within[:, None, :]
    decay = jnp.where(causal, jnp.exp(jnp.minimum(spread, 0.0)), 0.0)
    scores = jnp.einsum("shd,thd->hst", q, k, preferred_element_type=F32)
    weights = (scores * decay).astype(BF16)
    intra = jnp.einsum("hst,thd->shd", weights, v, preferred_element_type=F32)

    shape = (heads, quads * rows, DH)
    incs = got[:, :slab].reshape((inner,) + shape).astype(F32)
    upto, mixing = mixer(join3(jnp.moveaxis(got[:, slab : slab + 3, :heads], 1, 0)))
    local = jnp.sum(mixing[:, :, :, None, None] * incs[None], axis=1)

    total_log = jnp.pad(split3(upto[inner]), ((0, 5), (0, DH - heads)))
    total = jnp.concatenate([local[inner].reshape(slab, DH).astype(BF16), total_log])
    totals = lax.all_to_all(
        jnp.broadcast_to(total[None], (quads,) + total.shape), "za", 0, 0, tiled=True
    ).astype(F32)
    after, across = mixer(join3(jnp.moveaxis(totals[:, slab : slab + 3, :heads], 1, 0)))
    first = lax.dynamic_index_in_dim(
        state_in.reshape(heads, quads, inner, rows, DH), lax.axis_index(INNER), 2, keepdims=False
    ).reshape(shape)
    quad = lax.axis_index("za")
    totals = totals[:, :slab].reshape((quads,) + shape)

    def bound(c):
        weigh = lax.dynamic_index_in_dim(across, c, 0, keepdims=False)[:, :, None, None]
        carried = jnp.exp(lax.dynamic_index_in_dim(after, c, 0, keepdims=False))[:, None, None]
        return jnp.sum(weigh * totals, axis=0) + carried * first

    opening = bound(quad)
    final = lax.dynamic_index_in_dim(
        bound(quads).reshape(heads, quads, rows, DH), quad, 1, keepdims=False
    )
    states = local[:inner] + jnp.exp(upto[:inner])[:, :, None, None] * opening[None]
    states = states.astype(BF16).reshape(inner, slab, DH)
    back = lax.all_to_all(states, INNER, 0, 0, tiled=True)
    start = back.reshape(inner, heads, quads, rows, DH).transpose(1, 2, 0, 3, 4)
    start = start.reshape(heads, DH, DH)

    inter = jnp.einsum("shd,hde->she", q, start, preferred_element_type=F32)
    inter = inter * jnp.exp(within_down)[:, :, None]
    attended = (intra + inter).reshape(tokens, heads * DH)
    squares = jnp.sum(attended * attended, axis=1)
    gained = attended * norm_gain

    message = jnp.concatenate([gained.astype(BF16), tail_of(squares, 16, heads * DH)])
    message = jnp.broadcast_to(message[None], (ny,) + message.shape)
    acts = lax.all_to_all(message, "y", 0, 0, tiled=True)
    squares = rows_of(acts[:, tokens:], tokens)
    mine = tail_of(squares, 8, DH)
    each = lax.all_to_all(jnp.broadcast_to(mine[None], (nx,) + mine.shape), "x", 0, 0, tiled=True)
    scale = lax.rsqrt(rows_of(each, tokens) / (H * DH) + EPSILON)
    normed = (attended * scale[:, None] * norm_gain).astype(BF16)
    at = lax.axis_index("y").astype(jnp.int32).reshape(1)
    shares = lax.all_to_all(project(acts, gathered, scale[None], at), "x", 0, 0, tiled=True)
    layer_out = jnp.sum(shares.astype(F32), axis=0).astype(BF16)
    return (normed, final, layer_out)


def solution(mesh):
    fine = Mesh(mesh.devices.reshape(4, 4, 2, 4, 4), CTX + TP)
    return jax.shard_map(
        per_device,
        mesh=fine,
        in_specs=(
            P(CTX, TP),
            P(CTX, TP),
            P(CTX, TP),
            P(TP, CTX),
            P(TP, None, None),
            P(TP),
            P(TP, CTX),
        ),
        out_specs=(P(CTX, TP), P(TP, CTX, None), P(CTX, TP)),
        check_vma=False,
    )
```

```python
import functools

import jax
import jax.numpy as jnp
from jax import lax
from jax.experimental import pallas as pl
from jax.experimental.pallas import tpu as pltpu
from jax.sharding import Mesh, PartitionSpec as P

H = 64
DH = 128
EPSILON = 1e-06
CTX = ("za", "zb", "core")
INNER = ("zb", "core")
TP = ("x", "y")
FLIGHT = 6
HIGH = lax.Precision.HIGHEST
BF16 = jnp.bfloat16
F32 = jnp.float32


def split3(x):
    hi = lax.reduce_precision(x, 8, 7)
    rest = x - hi
    mid = lax.reduce_precision(rest, 8, 7)
    low = rest - mid
    return jnp.stack([hi.astype(BF16), mid.astype(BF16), low.astype(BF16)])


def join3(parts):
    parts = parts.astype(F32)
    return parts[0] + (parts[1] + parts[2])


def tail_of(vector, rows, width):
    flat = split3(vector).reshape(-1)
    return jnp.pad(flat, (0, rows * width - flat.shape[0])).reshape(rows, width)


def rows_of(tail, n):
    count = tail.shape[0]
    flat = tail.reshape(count, -1)[:, : 3 * n].reshape(count, 3, n)
    return jnp.sum(join3(jnp.moveaxis(flat, 1, 0)), axis=0)


def mixer(logs):
    count, heads = logs.shape
    upto = jnp.concatenate([jnp.zeros((1, heads), F32), jnp.cumsum(logs, axis=0)])
    before = jnp.arange(count)[None, :] < jnp.arange(count + 1)[:, None]
    gap = upto[:, None] - upto[None, 1:]
    factor = jnp.where(before[:, :, None], jnp.exp(jnp.minimum(gap, 0.0)), 0.0)
    return upto, factor


def z_step(y, core):
    return (0, 1, 2 - 4 * core, -1)[y]


def project_kernel(at_ref, acts_ref, weights_ref, scale_ref, out_ref, right, sems):
    tokens = scale_ref.shape[0]
    ny = acts_ref.shape[0]
    chips, cores, share, _ = weights_ref.shape
    y = at_ref[0]
    copies = []
    for n in range(chips // ny):
        for i in range(ny):
            group = []
            for c in range(cores):
                z = lax.rem(n * ny + y + chips + z_step(i, c), chips)
                part = right.at[n, i, pl.ds(c * share, share)]
                group.append(pltpu.make_async_copy(weights_ref.at[z, c], part, sems.at[n, i, c]))
            copies.append(group)
    for group in copies[:FLIGHT]:
        for copy in group:
            copy.start()
    m = 0
    for n in range(chips // ny):
        total = None
        for i in range(ny):
            for copy in copies[m]:
                copy.wait()
            if m + FLIGHT < len(copies):
                for copy in copies[m + FLIGHT]:
                    copy.start()
            m += 1
            value = lax.dot_general(
                acts_ref[i, :tokens, :],
                right[n, i],
                (((1,), (1,)), ((), ())),
                preferred_element_type=F32,
            )
            total = value if total is None else total + value
        out_ref[n] = (total * scale_ref[...]).astype(BF16)


def project(acts, weights, scale, at):
    ny, _, depth = acts.shape
    rows = scale.shape[0]
    chips, cores, share, _ = weights.shape
    nx, cols = chips // ny, cores * share
    vmem = pl.BlockSpec(memory_space=pltpu.VMEM)
    return pl.pallas_call(
        project_kernel,
        out_shape=pltpu.VMEM((nx, rows, cols), BF16),
        grid_spec=pltpu.PrefetchScalarGridSpec(
            num_scalar_prefetch=1,
            grid=(),
            in_specs=[vmem, pl.BlockSpec(memory_space=pl.ANY), vmem],
            out_specs=vmem,
            scratch_shapes=[
                pltpu.VMEM((nx, ny, cols, depth), BF16),
                pltpu.SemaphoreType.DMA((nx, ny, cores)),
            ],
        ),
        name="project",
    )(at, pltpu.with_memory_space_constraint(acts, pltpu.VMEM), weights, scale)


def open_kernel(quads, keep_ref, keys_ref, values_ref, message_ref, across_ref, down_ref):
    tokens = keys_ref.shape[0]
    heads = keep_ref.shape[0]
    inner = message_ref.shape[0]
    each = DH // inner
    step = each // quads
    row = lax.broadcasted_iota(jnp.int32, (tokens, tokens), 0)
    col = lax.broadcasted_iota(jnp.int32, (tokens, tokens), 1)
    sums = (col <= row).astype(F32)
    keep = keep_ref[...]
    down = lax.dot_general(sums, keep, (((1,), (1,)), ((), ())), precision=HIGH, preferred_element_type=F32)
    across_ref[...] = lax.dot_general(
        keep, sums, (((1,), (1,)), ((), ())), precision=HIGH, preferred_element_type=F32
    )
    down_ref[...] = down
    last = down[tokens - 1 :, :]
    factor = jnp.exp(last - down)
    to = lax.broadcasted_iota(jnp.int32, (DH, DH), 0)
    of = lax.broadcasted_iota(jnp.int32, (DH, DH), 1)
    wanted = (to % each) // step * (inner * step) + to // each * step + to % step
    order = (of == wanted).astype(BF16)
    for h in range(heads):
        span = slice(h * DH, (h + 1) * DH)
        decayed = (keys_ref[:, span].astype(F32) * factor[:, h : h + 1]).astype(BF16)
        inc = lax.dot_general(
            decayed, values_ref[:, span], (((0,), (0,)), ((), ())), preferred_element_type=F32
        )
        inc = jnp.dot(order, inc.astype(BF16), preferred_element_type=F32).astype(BF16)
        for i in range(inner):
            message_ref[i, h * each : (h + 1) * each, :] = inc[i * each : (i + 1) * each, :]
    lane = lax.broadcasted_iota(jnp.int32, (8, DH), 1)
    line = lax.broadcasted_iota(jnp.int32, (8, DH), 0)
    logs = jnp.zeros((8, DH), F32)
    for h in range(heads):
        logs = jnp.where(lane == h, last[:, h : h + 1], logs)
    hi = logs.astype(BF16).astype(F32)
    mid = (logs - hi).astype(BF16).astype(F32)
    low = logs - hi - mid
    logs = jnp.where(line == 0, hi, jnp.where(line == 1, mid, jnp.where(line == 2, low, 0.0)))
    for i in range(inner):
        message_ref[i, heads * each :, :] = logs.astype(BF16)


def open_scan(log_keep, keys, values, quads, inner):
    heads, tokens = log_keep.shape
    vmem = pl.BlockSpec(memory_space=pltpu.VMEM)
    return pl.pallas_call(
        functools.partial(open_kernel, quads),
        out_shape=[
            jax.ShapeDtypeStruct((inner, heads * DH // inner + 8, DH), BF16),
            jax.ShapeDtypeStruct((heads, tokens), F32),
            jax.ShapeDtypeStruct((tokens, heads), F32),
        ],
        in_specs=[vmem] * 3,
        out_specs=[vmem] * 3,
        name="open_scan",
    )(log_keep, keys, values)


def per_device(queries, keys, values, log_keep, state_in, norm_gain, out_weight):
    tokens = queries.shape[0]
    heads = log_keep.shape[0]
    parts = lax.axis_size(CTX)
    quads, inner = lax.axis_size("za"), lax.axis_size(INNER)
    rows = DH // parts
    slab = heads * quads * rows
    nx, ny = lax.axis_size("x"), lax.axis_size("y")

    cores = lax.axis_size("core")
    chips = parts // cores
    swap = [
        (
            (z * cores + c) * ny + y,
            ((z + z_step(y, c)) % chips * cores + c) * ny + z % ny,
        )
        for z in range(chips)
        for c in range(cores)
        for y in range(ny)
    ]
    moved = lax.ppermute(out_weight.T, CTX + ("y",), swap)

    q = queries.reshape(tokens, heads, DH)
    k = keys.reshape(tokens, heads, DH)
    v = values.reshape(tokens, heads, DH)
    opener, within, within_down = open_scan(log_keep, keys, values, quads, inner)
    got = lax.all_to_all(opener, INNER, 0, 0, tiled=True)

    moved, opener = lax.optimization_barrier((moved, opener))
    gathered = lax.all_gather(moved, CTX, axis=0, tiled=True)
    cols = out_weight.shape[1] * parts // (nx * ny)
    gathered = gathered.reshape(chips, cores, cols // cores, out_weight.shape[0])

    causal = jnp.tril(jnp.ones((tokens, tokens), dtype=bool))
    spread = within[:, :, None] - within[:, None, :]
    decay = jnp.where(causal, jnp.exp(jnp.minimum(spread, 0.0)), 0.0)
    scores = jnp.einsum("shd,thd->hst", q, k, preferred_element_type=F32)
    weights = (scores * decay).astype(BF16)
    intra = jnp.einsum("hst,thd->shd", weights, v, preferred_element_type=F32)

    shape = (heads, quads * rows, DH)
    incs = got[:, :slab].reshape((inner,) + shape).astype(F32)
    upto, mixing = mixer(join3(jnp.moveaxis(got[:, slab : slab + 3, :heads], 1, 0)))
    local = jnp.sum(mixing[:, :, :, None, None] * incs[None], axis=1)

    total_log = jnp.pad(split3(upto[inner]), ((0, 5), (0, DH - heads)))
    total = jnp.concatenate([local[inner].reshape(slab, DH).astype(BF16), total_log])
    totals = lax.all_to_all(
        jnp.broadcast_to(total[None], (quads,) + total.shape), "za", 0, 0, tiled=True
    ).astype(F32)
    after, across = mixer(join3(jnp.moveaxis(totals[:, slab : slab + 3, :heads], 1, 0)))
    first = lax.dynamic_index_in_dim(
        state_in.reshape(heads, quads, inner, rows, DH), lax.axis_index(INNER), 2, keepdims=False
    ).reshape(shape)
    quad = lax.axis_index("za")
    totals = totals[:, :slab].reshape((quads,) + shape)

    def bound(c):
        weigh = lax.dynamic_index_in_dim(across, c, 0, keepdims=False)[:, :, None, None]
        carried = jnp.exp(lax.dynamic_index_in_dim(after, c, 0, keepdims=False))[:, None, None]
        return jnp.sum(weigh * totals, axis=0) + carried * first

    opening = bound(quad)
    final = lax.dynamic_index_in_dim(
        bound(quads).reshape(heads, quads, rows, DH), quad, 1, keepdims=False
    )
    states = local[:inner] + jnp.exp(upto[:inner])[:, :, None, None] * opening[None]
    states = states.astype(BF16).reshape(inner, slab, DH)
    back = lax.all_to_all(states, INNER, 0, 0, tiled=True)
    start = back.reshape(inner, heads, quads, rows, DH).transpose(1, 2, 0, 3, 4)
    start = start.reshape(heads, DH, DH)

    inter = jnp.einsum("shd,hde->she", q, start, preferred_element_type=F32)
    inter = inter * jnp.exp(within_down)[:, :, None]
    attended = (intra + inter).reshape(tokens, heads * DH)
    squares = jnp.sum(attended * attended, axis=1)
    gained = attended * norm_gain

    message = jnp.concatenate([gained.astype(BF16), tail_of(squares, 16, heads * DH)])
    message = jnp.broadcast_to(message[None], (ny,) + message.shape)
    acts = lax.all_to_all(message, "y", 0, 0, tiled=True)
    squares = rows_of(acts[:, tokens:], tokens)
    mine = tail_of(squares, 8, DH)
    each = lax.all_to_all(jnp.broadcast_to(mine[None], (nx,) + mine.shape), "x", 0, 0, tiled=True)
    scale = lax.rsqrt(rows_of(each, tokens) / (H * DH) + EPSILON)
    normed = (attended * scale[:, None] * norm_gain).astype(BF16)
    at = lax.axis_index("y").astype(jnp.int32).reshape(1)
    shares = lax.all_to_all(project(acts, gathered, scale[:, None], at), "x", 0, 0, tiled=True)
    layer_out = jnp.sum(shares.astype(F32), axis=0).astype(BF16)
    return (normed, final, layer_out)


def solution(mesh):
    fine = Mesh(mesh.devices.reshape(4, 4, 2, 4, 4), CTX + TP)
    return jax.shard_map(
        per_device,
        mesh=fine,
        in_specs=(
            P(CTX, TP),
            P(CTX, TP),
            P(CTX, TP),
            P(TP, CTX),
            P(TP, None, None),
            P(TP),
            P(TP, CTX),
        ),
        out_specs=(P(CTX, TP), P(TP, CTX, None), P(CTX, TP)),
        check_vma=False,
    )
```
